32 devices in a mesh: gx: 2 (over x), gy: 4 (over y, core), gz: 4 (over z).
Axes of the slice: x: 2, y: 2, z: 4, core: 2. Of those that a mesh axis runs over, the one named last changes fastest.
Arguments:
- fluidity: float32 [16, 192, 1024], P('gx', 'gy', 'gz'), may hold values from -6 to 6
- local_fluidity: float32 [16, 192, 1024], P('gx', 'gy', 'gz'), may hold values from -12 to 18
- element_coef: float32 [2, 24, 128], P('gx', 'gy', 'gz'), may hold values from 0.2 to 2
- fdm_basis: float32 [8, 8], replicated, may hold values from -2 to 2
- fdm_values: float32 [8], replicated, may hold values from 0.5 to 40
- coarse_inverse: float32 [32, 32], P(('gx', 'gy', 'gz')), may hold values from -1 to 1
Outputs:
- correction: float32 [16, 192, 1024], P('gx', 'gy', 'gz')
The draws below stay inside these ranges and needn't reach their ends.
All inputs are finite; a program needn't handle non-finite values.
Results may differ from the reference program's by a relative error of at most 0.0001.
Values sent between devices are 32-bit elements; how exact they have to be, the bound alone decides.
No kernel may reach another device: no remote copies, remote signals or barrier semaphores. Data moves between devices by JAX's collectives and lax.ppermute only.
A program may use at most 64 MiB of HBM per device.

```python
import math
import jax
import jax.numpy as jnp
import numpy as np
from jax import lax

NP = 8
EX = 1
PX = 8
PY = 48
PZ = 256
EXG = 2
EYG = 24
EZG = 128
NPX = 16
NPY = 192
NPZ = 1024
N_GX = 2
N_GY = 4
N_GZ = 4
DEVICES = 32


def position_fraction(length, elements):
    position = jnp.arange(length)
    element_index = (position // NP).astype(jnp.float32)
    local_node = (position % NP).astype(jnp.float32)
    return (element_index + local_node / (NP - 1)) / elements


def draw_local_fluidity(key, part):
    first_key = jax.random.fold_in(key, 0)
    shape_all = (NPX, NPY, NPZ)
    radial = position_fraction(NPX, EXG)[:, None, None]
    beside_all = position_fraction(NPY, EYG)[None, :, None]
    height = position_fraction(NPZ, EZG)[None, None, :]
    smooth = 0.6 * (1.0 + 2.0 * radial) * (1.5 + jnp.cos(2.0 * math.pi * beside_all)) * (0.5 + height)
    random_part = jnp.clip(jax.random.normal(first_key, shape_all, jnp.float32), -5.0, 5.0)
    return random_part + smooth


def block_levels(rng, dims, pieces, low, top_value):
    loudness = 1.0
    for axis_at, parts in pieces:
        heights = jax.random.uniform(jax.random.fold_in(jax.random.fold_in(rng, 6), axis_at), (parts,), jnp.float32, low / len(pieces), top_value / len(pieces))
        loudness = loudness * jnp.repeat(jnp.exp(heights), dims[axis_at] // parts).reshape((-1,) + (1,) * (len(dims) - 1 - axis_at))
    return loudness


def noise(own_key, shape, spread, most, cuts=(), kind=jnp.bfloat16):
    result = jax.random.normal(own_key, shape, jnp.float32) * spread
    if len(cuts) > 0:
        result = block_levels(own_key, shape, cuts, -0.22, 0.18) * result
    return jnp.clip(result, min=-most, max=most).astype(kind)


def setup_inputs(seed: int = 0) -> dict:
    seeds = jax.random.split(jax.random.key(seed), 7)
    return {
        "fluidity": noise(seeds[0], (NPX, NPY, NPZ), 1.0, 6.0, ((0, 2), (1, 4), (2, 4)), jnp.float32),
        "local_fluidity": draw_local_fluidity(jax.random.fold_in(seeds[6], 71), 0),
        "element_coef": jnp.clip(jnp.exp(math.log(2.0) - 2.3025851 * jax.random.uniform(seeds[2], (EXG, EYG, EZG), jnp.float32) ** block_levels(seeds[2], (EXG, EYG, EZG), ((0, 2), (1, 4), (2, 4)), -0.2, 0.2)), 0.2, 2.0),
        "fdm_basis": noise(seeds[3], (NP, NP), NP ** -0.5, 2.0, (), jnp.float32),
        "fdm_values": jnp.clip(jnp.exp(jax.random.uniform(seeds[4], (NP,), jnp.float32, math.log(0.5), math.log(40.0))), 0.5, 40.0),
        "coarse_inverse": noise(seeds[5], (DEVICES, DEVICES), DEVICES ** -0.5, 1.0, ((0, 32),), jnp.float32),
    }


HALF_WIDTH = 3.0
HIGHEST = lax.Precision.HIGHEST
GLL_EIGHT = (-1.0, -0.8717401485096066, -0.5917001814331423, -0.2092992179024789, 0.2092992179024789, 0.5917001814331423, 0.8717401485096066, 1.0)


def gll_tables():
    degree = NP - 1
    gll_nodes = np.array(GLL_EIGHT)
    previous = np.ones(NP)
    current = gll_nodes * 1.0
    for order in range(2, degree + 1):
        following = ((2 * order - 1) * gll_nodes * current - (order - 1) * previous) / order
        previous = current
        current = following
    at_nodes = current
    weights = 2.0 / (degree * (degree + 1) * at_nodes * at_nodes)
    identity = np.eye(NP)
    spacing = gll_nodes[:, None] - gll_nodes[None, :] + identity
    derivative = at_nodes[:, None] / at_nodes[None, :] / spacing * (1.0 - identity)
    end_value = degree * (degree + 1) / 4.0
    end_values = np.concatenate([np.array([-end_value]), np.zeros(NP - 2), np.array([end_value])])
    derivative = derivative + identity * end_values[None, :]
    return jnp.asarray(weights, dtype=jnp.float32), jnp.asarray(derivative, dtype=jnp.float32)


def share_vector(length):
    position = jnp.arange(length) % NP
    return jnp.where((position == 0) | (position == NP - 1), 1.0, 2.0).astype(jnp.float32) ** -1


def slice_along(tensor, dimension, window):
    index_list = [slice(None)] * tensor.ndim
    index_list[dimension] = window
    return tensor[tuple(index_list)]


def fold_dimension(padded, dimension):
    length = padded.shape[dimension] - 2
    middle = slice_along(padded, dimension, slice(1, length + 1))
    before = slice_along(padded, dimension, slice(0, length))
    beyond = slice_along(padded, dimension, slice(2, length + 2))
    bcast_shape = [1] * padded.ndim
    bcast_shape[dimension] = length
    position = (jnp.arange(length) % NP).reshape(bcast_shape)
    return middle + jnp.where(position == 0, before, 0.0) + jnp.where(position == NP - 1, beyond, 0.0)


def assemble(padded):
    return fold_dimension(fold_dimension(fold_dimension(padded, 0), 1), 2)


def apply_matrix(matrix, tensor, dimension):
    shape_in = tensor.shape
    split_shape = shape_in[:dimension] + (shape_in[dimension] // NP, NP) + shape_in[dimension + 1:]
    product = jnp.tensordot(tensor.reshape(split_shape), matrix, axes=([dimension + 1], [1]), precision=HIGHEST)
    return jnp.moveaxis(product, -1, dimension + 1).reshape(shape_in)


def expand_coef(coeffs):
    return jnp.repeat(jnp.repeat(jnp.repeat(coeffs, NP, 0), NP, 1), NP, 2)


def element_terms(current, target, coef_field, weights, derivative):
    size_x, size_y, size_z = current.shape
    mass_diag = jnp.tile(weights, size_x // NP)[:, None, None] * jnp.tile(weights, size_y // NP)[None, :, None] * jnp.tile(weights, size_z // NP)[None, None, :]
    flux_scale = mass_diag * coef_field
    stiffness = jnp.zeros(current.shape, jnp.float32)
    for dimension in range(3):
        gradient = apply_matrix(derivative, current, dimension)
        stiffness = stiffness + apply_matrix(derivative.T, flux_scale * gradient, dimension)
    return HALF_WIDTH ** 3 * mass_diag * (target - current) - HALF_WIDTH * stiffness


def fdm_solve(residual, coef_field, fdm_basis, fdm_values):
    size_x, size_y, size_z = residual.shape
    spectra = jnp.tile(fdm_values, size_x // NP)[:, None, None] + jnp.tile(fdm_values, size_y // NP)[None, :, None] + jnp.tile(fdm_values, size_z // NP)[None, None, :]
    transformed = residual
    for dimension in range(3):
        transformed = apply_matrix(fdm_basis.T, transformed, dimension)
    transformed = transformed / (coef_field * spectra + 1.0)
    for dimension in range(3):
        transformed = apply_matrix(fdm_basis, transformed, dimension)
    return transformed


def pad_global(tensor):
    padded = jnp.pad(tensor, ((1, 1), (0, 0), (1, 1)))
    return jnp.concatenate([padded[:, -1:], padded, padded[:, :1]], axis=1)


def reference(fluidity, local_fluidity, element_coef, fdm_basis, fdm_values, coarse_inverse):
    weights, derivative = gll_tables()
    slab_shape = (EXG, NP, NPY, NPZ)

    def slab_terms(inputs):
        current, target, coeffs = inputs
        return element_terms(current, target, expand_coef(coeffs[None]), weights, derivative)

    local_terms = lax.map(slab_terms, (fluidity.reshape(slab_shape), local_fluidity.reshape(slab_shape), element_coef)).reshape(NPX, NPY, NPZ)
    index_x = jnp.arange(NPX)
    index_z = jnp.arange(NPZ)
    keep_x = ((index_x > 0) & (index_x < NPX - 1)).astype(jnp.float32)
    keep_z = ((index_z > 0) & (index_z < NPZ - 1)).astype(jnp.float32)
    mask = keep_x[:, None, None] * keep_z[None, None, :]
    residual = assemble(pad_global(local_terms)) * mask
    coarse_rhs = jnp.einsum('aibjck,i,j,k->abc', residual.reshape(N_GX, PX, N_GY, PY, N_GZ, PZ), share_vector(PX), share_vector(PY), share_vector(PZ), precision=HIGHEST) / (PX * PY * PZ)
    coarse_solution = jnp.dot(coarse_inverse, coarse_rhs.reshape(-1), precision=HIGHEST).reshape(N_GX, N_GY, N_GZ)
    coarse_rows = jnp.repeat(coarse_solution, EX, 0)
    share_slab = share_vector(NP)[:, None, None] * share_vector(NPY)[None, :, None] * share_vector(NPZ)[None, None, :]

    def slab_solve(inputs):
        resid_slab, coeffs, coarse_row = inputs
        solved = fdm_solve(resid_slab, expand_coef(coeffs[None]), fdm_basis, fdm_values)
        coarse_slab = jnp.repeat(jnp.repeat(coarse_row, PY, 0), PZ, 1)[None]
        return solved + share_slab * coarse_slab

    combined = lax.map(slab_solve, (residual.reshape(slab_shape), element_coef, coarse_rows)).reshape(NPX, NPY, NPZ)
    return assemble(pad_global(combined)) * mask
```

```python
import functools

import jax
import jax.numpy as jnp
import numpy as np
from jax import lax
from jax.experimental import pallas as pl
from jax.experimental.pallas import tpu as pltpu
from jax.sharding import PartitionSpec as P

NP = 8
HALF_WIDTH = 3.0
HIGHEST = lax.Precision.HIGHEST
AXES = ("gx", "gy", "gz")
LANES = 128
GLL_EIGHT = (
    -1.0,
    -0.8717401485096066,
    -0.5917001814331423,
    -0.2092992179024789,
    0.2092992179024789,
    0.5917001814331423,
    0.8717401485096066,
    1.0,
)


def gll_tables():
    degree = NP - 1
    gll_nodes = np.array(GLL_EIGHT)
    previous = np.ones(NP)
    current = gll_nodes * 1.0
    for order in range(2, degree + 1):
        following = ((2 * order - 1) * gll_nodes * current - (order - 1) * previous) / order
        previous = current
        current = following
    weights = 2.0 / (degree * (degree + 1) * current * current)
    identity = np.eye(NP)
    spacing = gll_nodes[:, None] - gll_nodes[None, :] + identity
    derivative = current[:, None] / current[None, :] / spacing * (1.0 - identity)
    end_value = degree * (degree + 1) / 4.0
    end_values = np.concatenate([np.array([-end_value]), np.zeros(NP - 2), np.array([end_value])])
    return weights, derivative + identity * end_values[None, :]


WEIGHTS, DERIVATIVE = gll_tables()
STIFF = (DERIVATIVE.T * WEIGHTS[None, :]) @ DERIVATIVE / WEIGHTS[:, None]


def dot(a, b, contract=((1,), (0,))):
    return lax.dot_general(
        a, b, (contract, ((), ())), precision=HIGHEST, preferred_element_type=jnp.float32
    )


def iota(shape, dim):
    return lax.broadcasted_iota(jnp.int32, shape, dim)


def is_even(axis):
    return lax.rem(lax.axis_index(axis), 2) == 0


def is_last(axis):
    return lax.axis_index(axis) == lax.axis_size(axis) - 1


def low_high(received, axis):
    if len(received) == 1:
        return received[0], received[0]
    even = is_even(axis)
    return jnp.where(even, received[1], received[0]), jnp.where(even, received[0], received[1])


def pair_payloads(low, high, axis, count):
    even = is_even(axis)
    payloads = [jnp.where(even, high, low)]
    if count > 1:
        payloads.append(jnp.where(even, low, high))
    return payloads


def merge(own, received):
    return jnp.where(own == 0.0, received, own)


def coarse_weight(position, length, first, last, offset):
    node = position % NP
    edge = (node == 0) | (node == NP - 1)
    at_low, at_high = position == 0, position == length - 1
    own = jnp.where(edge, jnp.where(at_low | at_high, 1.0, 2.0), 0.5)
    own = jnp.where((at_low & first) | (at_high & last), 0.0, own)
    low = jnp.where(at_low & jnp.logical_not(first), 1.0, 0.0)
    high = jnp.where(at_high & jnp.logical_not(last), 1.0, 0.0)
    return jnp.where(offset == 0, own, jnp.where(offset < 0, low, high))


def never():
    return jnp.bool_(False)


def z_weights(length, block, shape, position_dim):
    k = lax.axis_index("gz")
    offset = block - k
    value = coarse_weight(iota(shape, position_dim), length, k == 0, is_last("gz"), offset)
    return jnp.where(jnp.abs(offset) <= 1, value, 0.0)


def xy_weights(length_y, shape, y_dim, place, at_x, size_x):
    count = lax.axis_size("gy")
    i, j = lax.axis_index("gx"), lax.axis_index("gy")
    off_x = place // count - i
    off_y = lax.rem(place % count - j + count + 1, count) - 1
    y = coarse_weight(iota(shape, y_dim), length_y, False, False, off_y)
    x = coarse_weight(
        jnp.full(shape, at_x, jnp.int32), size_x, i == 0, is_last("gx"), off_x
    )
    return jnp.where((jnp.abs(off_x) <= 1) & (jnp.abs(off_y) <= 1), x * y, 0.0)


def store_faces(field_ref, yf_ref, zf_ref):
    size_x, size_y, size_z = field_ref.shape
    lane = iota((size_y, LANES), 1)
    low = jnp.zeros((size_y, LANES), jnp.float32)
    high = low
    for x in range(size_x):
        yf_ref[0, x : x + 1, :] = field_ref[x, 0:1, :]
        yf_ref[1, x : x + 1, :] = field_ref[x, size_y - 1 : size_y, :]
        low = jnp.where(lane == x, field_ref[x, :, 0:1], low)
        high = jnp.where(lane == x, field_ref[x, :, size_z - 1 : size_z], high)
    zf_ref[0] = low
    zf_ref[1] = high


def terms_kernel(gossip, pairs_x, u_ref, l_ref, coef_ref, cinv_ref, const_ref, t_ref, yf_ref, zf_ref, *outs):
    size_x, size_y, size_z = u_ref.shape
    x_refs = outs[:pairs_x]
    stiff_z = const_ref[0:size_z, :]
    stiff_y = const_ref[size_z : size_z + size_y, 0:size_y]
    mass = const_ref[size_z + size_y : size_z + size_y + NP, :]
    spread = (iota((size_z // NP, size_z), 0) == iota((size_z // NP, size_z), 1) // NP).astype(jnp.float32)
    coef = dot(coef_ref[0], spread) * HALF_WIDTH
    t_ref[...] = dot(u_ref[...].reshape(size_x * size_y, size_z), stiff_z).reshape(u_ref.shape)
    for x in range(size_x):
        t_ref[x] += dot(stiff_y, u_ref[x])
    for e in range(size_y // NP):
        rows = slice(e * NP, (e + 1) * NP)
        u = [u_ref[b, rows, :] for b in range(NP)]
        scale = coef[e : e + 1, :]
        for a in range(NP):
            total = t_ref[a, rows, :]
            for b in range(NP):
                total = total + float(STIFF[a, b]) * u[b]
            source = HALF_WIDTH**3 * (l_ref[a, rows, :] - u[a])
            t_ref[a, rows, :] = (float(WEIGHTS[a]) * mass) * (source - scale * total)
    store_faces(t_ref, yf_ref, zf_ref)
    faces = pair_payloads(t_ref[0], t_ref[size_x - 1], "gx", pairs_x)
    for ref, face in zip(x_refs, faces):
        ref[0:size_y, :] = face
    if gossip:
        tab = coarse_tables(t_ref, cinv_ref)
        outs[pairs_x][...] = tab
        x_refs[0][size_y:, :] = tab


def coarse_tables(t_ref, cinv_ref):
    size_x, size_y, size_z = t_ref.shape
    count_z = lax.axis_size("gz")
    rows = lax.axis_size("gx") * lax.axis_size("gy")
    device = (lax.axis_index("gx") * lax.axis_size("gy") + lax.axis_index("gy")) * count_z + lax.axis_index("gz")
    middle = t_ref[1]
    for x in range(2, size_x - 1):
        middle = middle + t_ref[x]
    total = jnp.zeros((rows, size_z), jnp.float32)
    for at_x, plane in ((0, t_ref[0]), (1, middle), (size_x - 1, t_ref[size_x - 1])):
        w = xy_weights(size_y, (rows, size_y), 1, iota((rows, size_y), 0), at_x, size_x)
        total = total + dot(w, plane)
    lane = iota((size_z, LANES), 1)
    w = z_weights(size_z, lane % count_z, (size_z, LANES), 0)
    points = size_x * size_y * size_z
    part = dot(total, jnp.where(lane // count_z == device, w, 0.0)) / points
    width = rows * count_z
    row = jnp.broadcast_to(cinv_ref[...], (rows, width))
    row = jnp.where(iota((rows, width), 1) // count_z == iota((rows, width), 0), row, 0.0)
    lane = iota((width, LANES), 1)
    place = (lane // count_z == device) & (lane % count_z == iota((width, LANES), 0) % count_z)
    inverse = dot(row, place.astype(jnp.float32))
    return jnp.concatenate([part, inverse], axis=1)


def coarse_planes(tab, size_x, size_y, size_z):
    count_z = lax.axis_size("gz")
    rows = tab.shape[0]
    same = (iota((LANES, LANES), 0) % count_z == iota((LANES, LANES), 1) % count_z).astype(jnp.float32)
    rhs = dot(tab[:, :LANES], same)
    value = jnp.sum(rhs * tab[:, LANES:], axis=0, keepdims=True)
    value = jnp.broadcast_to(value, (rows, LANES))
    value = jnp.where(iota((rows, LANES), 1) // (count_z * count_z) == iota((rows, LANES), 0), value, 0.0)
    shape = (LANES, size_z)
    line = dot(value, z_weights(size_z, (iota(shape, 0) // count_z) % count_z, shape, 1))
    planes = []
    for at_x in (0, 1, size_x - 1):
        w = xy_weights(size_y, (size_y, rows), 0, iota((size_y, rows), 1), at_x, size_x)
        planes.append(dot(w, line))
    return planes


def y_kernel(gossip, pairs_x, extra, yf_ref, tab_ref, *refs):
    size_x, size_z = yf_ref.shape[1:]
    x_refs, refs = refs[:pairs_x], refs[pairs_x:]
    extra_refs, refs = refs[:extra], refs[extra:]
    size_y = x_refs[0].shape[0] - (NP if gossip else 0)
    row = iota((size_x, size_z), 0)
    faces = []
    for side, at in ((0, 0), (1, size_y - 1)):
        x_low, x_high = low_high([r[at : at + 1, :] for r in x_refs], "gx")
        face = yf_ref[side]
        faces.append(face + jnp.where(row == 0, x_low, 0.0) + jnp.where(row == size_x - 1, x_high, 0.0))
    for ref, face in zip(refs, pair_payloads(faces[0], faces[1], "gy", 2)):
        ref[0:size_x, :] = face
    if gossip:
        tab = merge(tab_ref[...], x_refs[0][size_y:, :])
        for r in extra_refs:
            tab = merge(tab, r[...])
        refs[0][size_x:, :] = tab
        refs[1][size_x:, :] = tab
        refs[2][...] = tab


def z_kernel(gossip, pairs_x, zf_ref, tab_ref, *refs):
    size_y = zf_ref.shape[1]
    x_refs, y_refs, refs = refs[:pairs_x], refs[pairs_x : pairs_x + 2], refs[pairs_x + 2 :]
    size_x = y_refs[0].shape[0] - (NP if gossip else 0)
    size_z = y_refs[0].shape[1]
    lane = iota((size_y, LANES), 1)
    row = iota((size_y, LANES), 0)
    diagonal = iota((size_x, LANES), 0) == iota((size_x, LANES), 1)
    faces = []
    for side, at in ((0, 0), (1, size_z - 1)):
        x_low, x_high = low_high([r[0:size_y, at : at + 1] for r in x_refs], "gx")
        y_low, y_high = low_high([r[0:size_x, at : at + 1] for r in y_refs], "gy")
        face = zf_ref[side]
        face = face + jnp.where(lane == 0, x_low, 0.0) + jnp.where(lane == size_x - 1, x_high, 0.0)
        for at_y, column in ((0, y_low), (size_y - 1, y_high)):
            line = jnp.sum(jnp.where(diagonal, column, 0.0), axis=0, keepdims=True)
            face = face + jnp.where(row == at_y, line, 0.0)
        faces.append(face)
    for ref, face in zip(refs, pair_payloads(faces[0], faces[1], "gz", 2)):
        ref[0:size_y, :] = face
    if gossip:
        tab = tab_ref[...]
        for r in y_refs:
            tab = merge(tab, r[size_x:, :])
        for ref in refs[:2]:
            ref[size_y : size_y + NP, :] = tab[:, :LANES]
            ref[size_y + NP :, :] = tab[:, LANES:]
        refs[2][...] = tab


def with_halo(plane, x, size_x, x_halo, y_halo, z_halo):
    size_y, size_z = plane.shape
    if x == 0:
        plane = plane + x_halo[0]
    if x == size_x - 1:
        plane = plane + x_halo[1]
    row, lane = iota(plane.shape, 0), iota(plane.shape, 1)
    plane = plane + jnp.where(row == 0, y_halo[0][x : x + 1, :], 0.0)
    plane = plane + jnp.where(row == size_y - 1, y_halo[1][x : x + 1, :], 0.0)
    plane = plane + jnp.where(lane == 0, z_halo[0][:, x : x + 1], 0.0)
    plane = plane + jnp.where(lane == size_z - 1, z_halo[1][:, x : x + 1], 0.0)
    keep = jnp.logical_not(((lane == 0) & (lax.axis_index("gz") == 0)) | ((lane == size_z - 1) & is_last("gz")))
    if x == 0:
        keep = keep & (lax.axis_index("gx") != 0)
    if x == size_x - 1:
        keep = keep & jnp.logical_not(is_last("gx"))
    return jnp.where(keep, plane, 0.0)


def halos(shape, x_refs, y_refs, z_refs):
    size_x, size_y, _ = shape
    x_halo = low_high([r[0:size_y, :] for r in x_refs], "gx")
    y_halo = low_high([r[0:size_x, :] for r in y_refs], "gy")
    z_halo = low_high([r[0:size_y, :] for r in z_refs], "gz")
    return x_halo, y_halo, z_halo


def merged_table(tab_ref, z_refs, size_y):
    tab = tab_ref[...]
    for r in z_refs:
        tab = merge(tab, jnp.concatenate([r[size_y : size_y + NP, :], r[size_y + NP :, :]], axis=1))
    return tab


def prepare_kernel(basis_ref, values_ref, scalar_ref, coef_ref, pz_ref, pzt_ref, py_ref, pyt_ref, inv_ref):
    size_x, size_y, size_z = inv_ref.shape

    def folded(length, transposed):
        pick = (iota((length, NP), 0) % NP == iota((length, NP), 1)).astype(jnp.float32)
        basis = basis_ref[...]
        left = dot(pick, basis, ((1,), (1 if transposed else 0,)))
        wide = dot(left, pick, ((1,), (1,)))
        row, col = iota((length, length), 0), iota((length, length), 1)
        wide = jnp.where(row // NP == col // NP, wide, 0.0)
        dim, at = (1, col) if transposed else (0, row)
        after = pltpu.roll(wide, length - 1, dim)
        before = pltpu.roll(wide, 1, dim)
        wide = wide + jnp.where((at % NP == NP - 1) & (at != length - 1), after, 0.0)
        return wide + jnp.where((at % NP == 0) & (at != 0), before, 0.0)

    pz_ref[...] = folded(size_z, False)
    pzt_ref[...] = folded(size_z, True)
    py_ref[...] = folded(size_y, False)
    pyt_ref[...] = folded(size_y, True)
    spread = (iota((size_z // NP, size_z), 0) == iota((size_z // NP, size_z), 1) // NP).astype(jnp.float32)
    coef = dot(coef_ref[0], spread)
    pick = (iota((NP, size_z), 0) == iota((NP, size_z), 1) % NP).astype(jnp.float32)
    along_z = dot(values_ref[...], pick)
    diagonal = iota((NP, NP), 0) == iota((NP, NP), 1)
    along_y = jnp.sum(jnp.where(diagonal, values_ref[...], 0.0), axis=1, keepdims=True)
    along = along_y + along_z
    for e in range(size_y // NP):
        for a in range(NP):
            inv_ref[a, e * NP : (e + 1) * NP, :] = 1.0 / (coef[e : e + 1, :] * (along + scalar_ref[0, a]) + 1.0)


def solve_kernel(gossip, pairs_x, t_ref, basis_ref, pz_ref, pzt_ref, py_ref, pyt_ref, inv_ref, tab_ref, *refs):
    shape = size_x, size_y, size_z = t_ref.shape
    x_refs, y_refs, z_refs = refs[:pairs_x], refs[pairs_x : pairs_x + 2], refs[pairs_x + 2 : pairs_x + 4]
    y_ref, yf_ref, zf_ref, *outs = refs[pairs_x + 4 :]
    scratch = outs[-1]
    x_halo, y_halo, z_halo = halos(shape, x_refs, y_refs, z_refs)
    for x in range(size_x):
        plane = with_halo(t_ref[x], x, size_x, x_halo, y_halo, z_halo)
        y_ref[x] = dot(pyt_ref[...], plane)
    flat = (size_x * size_y, size_z)
    scratch[...] = dot(y_ref[...].reshape(flat), pz_ref[...]).reshape(shape)
    for e in range(size_y // NP):
        rows = slice(e * NP, (e + 1) * NP)
        r = [scratch[b, rows, :] for b in range(NP)]
        s = []
        for a in range(NP):
            total = basis_ref[0, a] * r[0]
            for b in range(1, NP):
                total = total + basis_ref[b, a] * r[b]
            s.append(total * inv_ref[a, rows, :])
        for a in range(NP):
            total = basis_ref[a, 0] * s[0]
            for b in range(1, NP):
                total = total + basis_ref[a, b] * s[b]
            scratch[a, rows, :] = total
    scratch[...] = dot(scratch[...].reshape(flat), pzt_ref[...]).reshape(shape)
    for x in range(size_x):
        y_ref[x] = dot(py_ref[...], scratch[x])
    store_faces(y_ref, yf_ref, zf_ref)
    for ref, face in zip(outs[:pairs_x], pair_payloads(y_ref[0], y_ref[size_x - 1], "gx", pairs_x)):
        ref[0:size_y, :] = face
    if gossip:
        tab = merged_table(tab_ref, z_refs, size_y)
        outs[pairs_x][...] = tab
        outs[0][size_y:, :] = tab


def final_kernel(gossip, pairs_x, s_ref, tab_ref, *refs):
    shape = size_x, size_y, size_z = s_ref.shape
    x_refs, y_refs, z_refs = refs[:pairs_x], refs[pairs_x : pairs_x + 2], refs[pairs_x + 2 : pairs_x + 4]
    out_ref = refs[-1]
    if gossip:
        coarse = coarse_planes(merged_table(tab_ref, z_refs, size_y), *shape)
    else:
        coarse = [tab_ref[c] for c in range(3)]
    x_halo, y_halo, z_halo = halos(shape, x_refs, y_refs, z_refs)
    for x in range(size_x):
        plane = s_ref[x] + coarse[0 if x == 0 else 2 if x == size_x - 1 else 1]
        out_ref[x] = with_halo(plane, x, size_x, x_halo, y_halo, z_halo)


VMEM = pl.BlockSpec(memory_space=pltpu.VMEM)
SMEM = pl.BlockSpec(memory_space=pltpu.SMEM)


def call(kernel, name, inputs, shapes, scratch=(), smem=()):
    return pl.pallas_call(
        kernel,
        name=name,
        out_shape=[jax.ShapeDtypeStruct(s, jnp.float32) for s in shapes],
        in_specs=[SMEM if n in smem else VMEM for n in range(len(inputs))],
        out_specs=[VMEM] * len(shapes),
        scratch_shapes=[pltpu.VMEM(s, jnp.float32) for s in scratch],
    )(*inputs)


def pair_permutations(sizes, dim):
    count = sizes[dim]
    result = []
    for odd in range(1 if count == 2 and dim != 1 else 2):
        pairs = []
        for place in np.ndindex(*sizes):
            other = list(place)
            step = 1 if place[dim] % 2 == odd else -1
            moved = place[dim] + step
            if dim == 1 or 0 <= moved < count:
                other[dim] = moved % count
            else:
                other[1] = place[1] ^ 1
            pairs.append((int(np.ravel_multi_index(place, sizes)), int(np.ravel_multi_index(other, sizes))))
        result.append(pairs)
    return result


def coarse_by_sums(terms, coarse_inverse):
    shape = terms.shape
    sides = []
    weights = []
    for dim, axis in enumerate(AXES):
        count, at = lax.axis_size(axis), lax.axis_index(axis)
        position = jnp.arange(shape[dim])
        first, last = (False, False) if dim == 1 else (at == 0, at == count - 1)
        weights.append(jnp.stack([coarse_weight(position, shape[dim], first, last, o) for o in (-1, 0, 1)]))
        block = at + jnp.arange(-1, 2)
        block = block % count if dim == 1 else block
        sides.append((block[:, None] == jnp.arange(count)[None, :]).astype(jnp.float32))
    part = jnp.einsum("xyz,ax,by,cz->abc", terms, *weights, precision=HIGHEST) / terms.size
    rhs = jnp.einsum("abc,ai,bj,ck->ijk", part, *sides, precision=HIGHEST)
    rhs = lax.psum(rhs, AXES)
    inverse = lax.all_gather(coarse_inverse, AXES, axis=0, tiled=True)
    value = jnp.dot(inverse, rhs.reshape(-1), precision=HIGHEST).reshape(rhs.shape)
    near = jnp.einsum("ijk,ai,bj,ck->abc", value, *sides, precision=HIGHEST)
    classes = weights[0][:, jnp.array([0, 1, shape[0] - 1])]
    return jnp.einsum("abc,ax,by,cz->xyz", near, classes, weights[1], weights[2], precision=HIGHEST)


def on_device(sizes, fluidity, local_fluidity, element_coef, fdm_basis, fdm_values, coarse_inverse):
    shape = size_x, size_y, size_z = fluidity.shape
    gossip = sizes == (2, 4, 4)
    extra_rows = NP if gossip else 0
    perms = [pair_permutations(sizes, dim) for dim in range(3)]
    pairs_x = len(perms[0])

    const = np.zeros((size_z + size_y + NP, size_z), np.float32)
    const[:size_z] = np.kron(np.eye(size_z // NP), STIFF.T)
    const[size_z : size_z + size_y, :size_y] = np.kron(np.eye(size_y // NP), STIFF)
    const[size_z + size_y :] = WEIGHTS[:, None] * np.tile(WEIGHTS, size_z // NP)[None, :]

    face_shapes = [(2, size_x, size_z), (2, size_y, LANES)]
    x_shapes = [(size_y + extra_rows, size_z)] * pairs_x
    tab_shapes = [(NP, size_z)] if gossip else []

    def send(payloads, pairs):
        return [lax.ppermute(p, AXES, q) for p, q in zip(payloads, pairs)]

    def exchange(y_faces, z_faces, x_payloads, tab, extra):
        x_got = send(x_payloads, perms[0])
        extra_got = send([tab] * len(extra), extra)
        y_out = call(
            functools.partial(y_kernel, gossip, pairs_x, len(extra)),
            "y_faces",
            [y_faces, tab, *x_got, *extra_got],
            [(size_x + extra_rows, size_z)] * 2 + tab_shapes,
        )
        y_got = send(y_out[:2], perms[1])
        tab = y_out[-1] if gossip else tab
        z_out = call(
            functools.partial(z_kernel, gossip, pairs_x),
            "z_faces",
            [z_faces, tab, *x_got, *y_got],
            [(size_y + 2 * extra_rows, LANES)] * 2 + tab_shapes,
        )
        z_got = send(z_out[:2], perms[2])
        tab = z_out[-1] if gossip else tab
        return [*x_got, *y_got, *z_got], tab

    terms, y_faces, z_faces, *rest = call(
        functools.partial(terms_kernel, gossip, pairs_x),
        "terms",
        [fluidity, local_fluidity, element_coef, coarse_inverse, const],
        [shape] + face_shapes + x_shapes + tab_shapes,
    )
    tab = rest[-1]
    extra = [perms[2][0]] if gossip else []
    got, tab = exchange(y_faces, z_faces, rest[:pairs_x], tab, extra)
    values = fdm_values.reshape(1, NP)
    operators = call(
        prepare_kernel,
        "operators",
        [fdm_basis, values, values, element_coef],
        [(size_z, size_z)] * 2 + [(size_y, size_y)] * 2 + [shape],
        smem=(2,),
    )
    solved, y_faces, z_faces, *rest = call(
        functools.partial(solve_kernel, gossip, pairs_x),
        "solve",
        [terms, fdm_basis, *operators, tab, *got],
        [shape] + face_shapes + x_shapes + tab_shapes,
        scratch=[shape],
        smem=(1,),
    )
    got, tab = exchange(y_faces, z_faces, rest[:pairs_x], rest[-1], [])
    coarse = tab if gossip else coarse_by_sums(terms, coarse_inverse)
    return call(
        functools.partial(final_kernel, gossip, pairs_x), "final", [solved, coarse, *got], [shape]
    )[0]


def solution(mesh):
    sizes = tuple(mesh.shape[axis] for axis in AXES)
    return jax.shard_map(
        functools.partial(on_device, sizes),
        mesh=mesh,
        in_specs=(
            P("gx", "gy", "gz"),
            P("gx", "gy", "gz"),
            P("gx", "gy", "gz"),
            P(),
            P(),
            P(("gx", "gy", "gz"), None),
        ),
        out_specs=P("gx", "gy", "gz"),
        check_vma=False,
    )
```

```python
import functools

import jax
import jax.numpy as jnp
import numpy as np
from jax import lax
from jax.experimental import pallas as pl
from jax.experimental.pallas import tpu as pltpu
from jax.sharding import PartitionSpec as P

NP = 8
HALF_WIDTH = 3.0
HIGHEST = lax.Precision.HIGHEST
AXES = ("gx", "gy", "gz")
LANES = 128
GLL_EIGHT = (
    -1.0,
    -0.8717401485096066,
    -0.5917001814331423,
    -0.2092992179024789,
    0.2092992179024789,
    0.5917001814331423,
    0.8717401485096066,
    1.0,
)


def gll_tables():
    degree = NP - 1
    gll_nodes = np.array(GLL_EIGHT)
    previous = np.ones(NP)
    current = gll_nodes * 1.0
    for order in range(2, degree + 1):
        following = ((2 * order - 1) * gll_nodes * current - (order - 1) * previous) / order
        previous = current
        current = following
    weights = 2.0 / (degree * (degree + 1) * current * current)
    identity = np.eye(NP)
    spacing = gll_nodes[:, None] - gll_nodes[None, :] + identity
    derivative = current[:, None] / current[None, :] / spacing * (1.0 - identity)
    end_value = degree * (degree + 1) / 4.0
    end_values = np.concatenate([np.array([-end_value]), np.zeros(NP - 2), np.array([end_value])])
    return weights, derivative + identity * end_values[None, :]


WEIGHTS, DERIVATIVE = gll_tables()
STIFF = (DERIVATIVE.T * WEIGHTS[None, :]) @ DERIVATIVE / WEIGHTS[:, None]


def dot(a, b, contract=((1,), (0,))):
    return lax.dot_general(
        a, b, (contract, ((), ())), precision=HIGHEST, preferred_element_type=jnp.float32
    )


def iota(shape, dim):
    return lax.broadcasted_iota(jnp.int32, shape, dim)


def is_even(axis):
    return lax.rem(lax.axis_index(axis), 2) == 0


def is_last(axis):
    return lax.axis_index(axis) == lax.axis_size(axis) - 1


def low_high(received, axis):
    if len(received) == 1:
        return received[0], received[0]
    even = is_even(axis)
    return jnp.where(even, received[1], received[0]), jnp.where(even, received[0], received[1])


def pair_payloads(low, high, axis, count):
    even = is_even(axis)
    payloads = [jnp.where(even, high, low)]
    if count > 1:
        payloads.append(jnp.where(even, low, high))
    return payloads


def merge(own, received):
    return jnp.where(own == 0.0, received, own)


def coarse_weight(position, length, first, last, offset):
    node = position % NP
    edge = (node == 0) | (node == NP - 1)
    at_low, at_high = position == 0, position == length - 1
    own = jnp.where(edge, jnp.where(at_low | at_high, 1.0, 2.0), 0.5)
    own = jnp.where((at_low & first) | (at_high & last), 0.0, own)
    low = jnp.where(at_low & jnp.logical_not(first), 1.0, 0.0)
    high = jnp.where(at_high & jnp.logical_not(last), 1.0, 0.0)
    return jnp.where(offset == 0, own, jnp.where(offset < 0, low, high))


def never():
    return jnp.bool_(False)


def z_weights(length, block, shape, position_dim):
    k = lax.axis_index("gz")
    offset = block - k
    value = coarse_weight(iota(shape, position_dim), length, k == 0, is_last("gz"), offset)
    return jnp.where(jnp.abs(offset) <= 1, value, 0.0)


def xy_weights(length_y, shape, y_dim, place, at_x, size_x):
    count = lax.axis_size("gy")
    i, j = lax.axis_index("gx"), lax.axis_index("gy")
    off_x = place // count - i
    off_y = lax.rem(place % count - j + count + 1, count) - 1
    y = coarse_weight(iota(shape, y_dim), length_y, False, False, off_y)
    x = coarse_weight(
        jnp.full(shape, at_x, jnp.int32), size_x, i == 0, is_last("gx"), off_x
    )
    return jnp.where((jnp.abs(off_x) <= 1) & (jnp.abs(off_y) <= 1), x * y, 0.0)


def store_faces(field_ref, yf_ref, zf_ref):
    size_x, size_y, size_z = field_ref.shape
    lane = iota((size_y, LANES), 1)
    low = jnp.zeros((size_y, LANES), jnp.float32)
    high = low
    for x in range(size_x):
        yf_ref[0, x : x + 1, :] = field_ref[x, 0:1, :]
        yf_ref[1, x : x + 1, :] = field_ref[x, size_y - 1 : size_y, :]
        low = jnp.where(lane == x, field_ref[x, :, 0:1], low)
        high = jnp.where(lane == x, field_ref[x, :, size_z - 1 : size_z], high)
    zf_ref[0] = low
    zf_ref[1] = high


def terms_kernel(gossip, pairs_x, u_ref, l_ref, coef_ref, cinv_ref, const_ref, t_ref, yf_ref, zf_ref, *outs):
    size_x, size_y, size_z = u_ref.shape
    x_refs = outs[:pairs_x]
    stiff_z = const_ref[0:size_z, :]
    stiff_y = const_ref[size_z : size_z + size_y, 0:size_y]
    mass = const_ref[size_z + size_y : size_z + size_y + NP, :]
    spread = (iota((size_z // NP, size_z), 0) == iota((size_z // NP, size_z), 1) // NP).astype(jnp.float32)
    coef = dot(coef_ref[0], spread) * HALF_WIDTH
    t_ref[...] = dot(u_ref[...].reshape(size_x * size_y, size_z), stiff_z).reshape(u_ref.shape)
    for x in range(size_x):
        t_ref[x] += dot(stiff_y, u_ref[x])
    for e in range(size_y // NP):
        rows = slice(e * NP, (e + 1) * NP)
        u = [u_ref[b, rows, :] for b in range(NP)]
        scale = coef[e : e + 1, :]
        for a in range(NP):
            total = t_ref[a, rows, :]
            for b in range(NP):
                total = total + float(STIFF[a, b]) * u[b]
            source = HALF_WIDTH**3 * (l_ref[a, rows, :] - u[a])
            t_ref[a, rows, :] = (float(WEIGHTS[a]) * mass) * (source - scale * total)
    store_faces(t_ref, yf_ref, zf_ref)
    faces = pair_payloads(t_ref[0], t_ref[size_x - 1], "gx", pairs_x)
    for ref, face in zip(x_refs, faces):
        ref[0:size_y, :] = face
    if gossip:
        tab = coarse_tables(t_ref, cinv_ref)
        outs[pairs_x][...] = tab
        x_refs[0][size_y:, :] = tab


def coarse_tables(t_ref, cinv_ref):
    size_x, size_y, size_z = t_ref.shape
    count_z = lax.axis_size("gz")
    rows = lax.axis_size("gx") * lax.axis_size("gy")
    device = (lax.axis_index("gx") * lax.axis_size("gy") + lax.axis_index("gy")) * count_z + lax.axis_index("gz")
    middle = t_ref[1]
    for x in range(2, size_x - 1):
        middle = middle + t_ref[x]
    total = jnp.zeros((rows, size_z), jnp.float32)
    for at_x, plane in ((0, t_ref[0]), (1, middle), (size_x - 1, t_ref[size_x - 1])):
        w = xy_weights(size_y, (rows, size_y), 1, iota((rows, size_y), 0), at_x, size_x)
        total = total + dot(w, plane)
    lane = iota((size_z, LANES), 1)
    w = z_weights(size_z, lane % count_z, (size_z, LANES), 0)
    points = size_x * size_y * size_z
    part = dot(total, jnp.where(lane // count_z == device, w, 0.0)) / points
    width = rows * count_z
    row = jnp.broadcast_to(cinv_ref[...], (rows, width))
    row = jnp.where(iota((rows, width), 1) // count_z == iota((rows, width), 0), row, 0.0)
    lane = iota((width, LANES), 1)
    place = (lane // count_z == device) & (lane % count_z == iota((width, LANES), 0) % count_z)
    inverse = dot(row, place.astype(jnp.float32))
    return jnp.concatenate([part, inverse], axis=1)


def coarse_planes(tab, size_x, size_y, size_z):
    count_z = lax.axis_size("gz")
    rows = tab.shape[0]
    same = (iota((LANES, LANES), 0) % count_z == iota((LANES, LANES), 1) % count_z).astype(jnp.float32)
    rhs = dot(tab[:, :LANES], same)
    value = jnp.sum(rhs * tab[:, LANES:], axis=0, keepdims=True)
    value = jnp.broadcast_to(value, (rows, LANES))
    value = jnp.where(iota((rows, LANES), 1) // (count_z * count_z) == iota((rows, LANES), 0), value, 0.0)
    shape = (LANES, size_z)
    line = dot(value, z_weights(size_z, (iota(shape, 0) // count_z) % count_z, shape, 1))
    planes = []
    for at_x in (0, 1, size_x - 1):
        w = xy_weights(size_y, (size_y, rows), 0, iota((size_y, rows), 1), at_x, size_x)
        planes.append(dot(w, line))
    return planes


def y_kernel(gossip, pairs_x, extra, yf_ref, tab_ref, *refs):
    size_x, size_z = yf_ref.shape[1:]
    x_refs, refs = refs[:pairs_x], refs[pairs_x:]
    extra_refs, refs = refs[:extra], refs[extra:]
    size_y = x_refs[0].shape[0] - (NP if gossip else 0)
    row = iota((size_x, size_z), 0)
    faces = []
    for side, at in ((0, 0), (1, size_y - 1)):
        x_low, x_high = low_high([r[at : at + 1, :] for r in x_refs], "gx")
        face = yf_ref[side]
        faces.append(face + jnp.where(row == 0, x_low, 0.0) + jnp.where(row == size_x - 1, x_high, 0.0))
    for ref, face in zip(refs, pair_payloads(faces[0], faces[1], "gy", 2)):
        ref[0:size_x, :] = face
    if gossip:
        tab = merge(tab_ref[...], x_refs[0][size_y:, :])
        for r in extra_refs:
            tab = merge(tab, r[...])
        refs[0][size_x:, :] = tab
        refs[1][size_x:, :] = tab
        refs[2][...] = tab


def z_kernel(gossip, pairs_x, zf_ref, tab_ref, *refs):
    size_y = zf_ref.shape[1]
    x_refs, y_refs, refs = refs[:pairs_x], refs[pairs_x : pairs_x + 2], refs[pairs_x + 2 :]
    size_x = y_refs[0].shape[0] - (NP if gossip else 0)
    size_z = y_refs[0].shape[1]
    lane = iota((size_y, LANES), 1)
    row = iota((size_y, LANES), 0)
    diagonal = iota((size_x, LANES), 0) == iota((size_x, LANES), 1)
    faces = []
    for side, at in ((0, 0), (1, size_z - 1)):
        x_low, x_high = low_high([r[0:size_y, at : at + 1] for r in x_refs], "gx")
        y_low, y_high = low_high([r[0:size_x, at : at + 1] for r in y_refs], "gy")
        face = zf_ref[side]
        face = face + jnp.where(lane == 0, x_low, 0.0) + jnp.where(lane == size_x - 1, x_high, 0.0)
        for at_y, column in ((0, y_low), (size_y - 1, y_high)):
            line = jnp.sum(jnp.where(diagonal, column, 0.0), axis=0, keepdims=True)
            face = face + jnp.where(row == at_y, line, 0.0)
        faces.append(face)
    for ref, face in zip(refs, pair_payloads(faces[0], faces[1], "gz", 2)):
        ref[0:size_y, :] = face
    if gossip:
        tab = tab_ref[...]
        for r in y_refs:
            tab = merge(tab, r[size_x:, :])
        for ref in refs[:2]:
            ref[size_y : size_y + NP, :] = tab[:, :LANES]
            ref[size_y + NP :, :] = tab[:, LANES:]
        refs[2][...] = tab


def with_halo(plane, x, size_x, x_halo, y_halo, z_halo):
    size_y, size_z = plane.shape
    if x == 0:
        plane = plane + x_halo[0]
    if x == size_x - 1:
        plane = plane + x_halo[1]
    row, lane = iota(plane.shape, 0), iota(plane.shape, 1)
    plane = plane + jnp.where(row == 0, y_halo[0][x : x + 1, :], 0.0)
    plane = plane + jnp.where(row == size_y - 1, y_halo[1][x : x + 1, :], 0.0)
    plane = plane + jnp.where(lane == 0, z_halo[0][:, x : x + 1], 0.0)
    plane = plane + jnp.where(lane == size_z - 1, z_halo[1][:, x : x + 1], 0.0)
    keep = jnp.logical_not(((lane == 0) & (lax.axis_index("gz") == 0)) | ((lane == size_z - 1) & is_last("gz")))
    if x == 0:
        keep = keep & (lax.axis_index("gx") != 0)
    if x == size_x - 1:
        keep = keep & jnp.logical_not(is_last("gx"))
    return jnp.where(keep, plane, 0.0)


def halos(shape, x_refs, y_refs, z_refs):
    size_x, size_y, _ = shape
    x_halo = low_high([r[0:size_y, :] for r in x_refs], "gx")
    y_halo = low_high([r[0:size_x, :] for r in y_refs], "gy")
    z_halo = low_high([r[0:size_y, :] for r in z_refs], "gz")
    return x_halo, y_halo, z_halo


def merged_table(tab_ref, z_refs, size_y):
    tab = tab_ref[...]
    for r in z_refs:
        tab = merge(tab, jnp.concatenate([r[size_y : size_y + NP, :], r[size_y + NP :, :]], axis=1))
    return tab


def prepare_kernel(basis_ref, values_ref, scalar_ref, coef_ref, pz_ref, pzt_ref, py_ref, pyt_ref, inv_ref):
    size_x, size_y, size_z = inv_ref.shape

    def folded(length, transposed):
        pick = (iota((length, NP), 0) % NP == iota((length, NP), 1)).astype(jnp.float32)
        basis = basis_ref[...]
        left = dot(pick, basis, ((1,), (1 if transposed else 0,)))
        wide = dot(left, pick, ((1,), (1,)))
        row, col = iota((length, length), 0), iota((length, length), 1)
        wide = jnp.where(row // NP == col // NP, wide, 0.0)
        dim, at = (1, col) if transposed else (0, row)
        after = pltpu.roll(wide, length - 1, dim)
        before = pltpu.roll(wide, 1, dim)
        wide = wide + jnp.where((at % NP == NP - 1) & (at != length - 1), after, 0.0)
        return wide + jnp.where((at % NP == 0) & (at != 0), before, 0.0)

    pz_ref[...] = folded(size_z, False)
    pzt_ref[...] = folded(size_z, True)
    py_ref[...] = folded(size_y, False)
    pyt_ref[...] = folded(size_y, True)
    spread = (iota((size_z // NP, size_z), 0) == iota((size_z // NP, size_z), 1) // NP).astype(jnp.float32)
    coef = dot(coef_ref[0], spread)
    pick = (iota((NP, size_z), 0) == iota((NP, size_z), 1) % NP).astype(jnp.float32)
    along_z = dot(values_ref[...], pick)
    diagonal = iota((NP, NP), 0) == iota((NP, NP), 1)
    along_y = jnp.sum(jnp.where(diagonal, values_ref[...], 0.0), axis=1, keepdims=True)
    along = along_y + along_z
    for e in range(size_y // NP):
        for a in range(NP):
            inv_ref[a, e * NP : (e + 1) * NP, :] = 1.0 / (coef[e : e + 1, :] * (along + scalar_ref[0, a]) + 1.0)


def solve_kernel(gossip, pairs_x, t_ref, basis_ref, pz_ref, pzt_ref, py_ref, pyt_ref, inv_ref, tab_ref, *refs):
    shape = size_x, size_y, size_z = t_ref.shape
    x_refs, y_refs, z_refs = refs[:pairs_x], refs[pairs_x : pairs_x + 2], refs[pairs_x + 2 : pairs_x + 4]
    y_ref, yf_ref, zf_ref, *outs = refs[pairs_x + 4 :]
    scratch = outs[-1]
    x_halo, y_halo, z_halo = halos(shape, x_refs, y_refs, z_refs)
    for x in range(size_x):
        plane = with_halo(t_ref[x], x, size_x, x_halo, y_halo, z_halo)
        y_ref[x] = dot(pyt_ref[...], plane)
    flat = (size_x * size_y, size_z)
    scratch[...] = dot(y_ref[...].reshape(flat), pz_ref[...]).reshape(shape)
    for e in range(size_y // NP):
        rows = slice(e * NP, (e + 1) * NP)
        r = [scratch[b, rows, :] for b in range(NP)]
        s = []
        for a in range(NP):
            total = basis_ref[0, a] * r[0]
            for b in range(1, NP):
                total = total + basis_ref[b, a] * r[b]
            s.append(total * inv_ref[a, rows, :])
        for a in range(NP):
            total = basis_ref[a, 0] * s[0]
            for b in range(1, NP):
                total = total + basis_ref[a, b] * s[b]
            scratch[a, rows, :] = total
    scratch[...] = dot(scratch[...].reshape(flat), pzt_ref[...]).reshape(shape)
    for x in range(size_x):
        y_ref[x] = dot(py_ref[...], scratch[x])
    store_faces(y_ref, yf_ref, zf_ref)
    for ref, face in zip(outs[:pairs_x], pair_payloads(y_ref[0], y_ref[size_x - 1], "gx", pairs_x)):
        ref[0:size_y, :] = face
    if gossip:
        tab = merged_table(tab_ref, z_refs, size_y)
        outs[pairs_x][...] = tab
        outs[0][size_y:, :] = tab


def final_kernel(gossip, pairs_x, s_ref, tab_ref, *refs):
    shape = size_x, size_y, size_z = s_ref.shape
    x_refs, y_refs, z_refs = refs[:pairs_x], refs[pairs_x : pairs_x + 2], refs[pairs_x + 2 : pairs_x + 4]
    out_ref = refs[-1]
    if gossip:
        coarse = coarse_planes(merged_table(tab_ref, z_refs, size_y), *shape)
    else:
        coarse = [tab_ref[c] for c in range(3)]
    x_halo, y_halo, z_halo = halos(shape, x_refs, y_refs, z_refs)
    for x in range(size_x):
        plane = s_ref[x] + coarse[0 if x == 0 else 2 if x == size_x - 1 else 1]
        out_ref[x] = with_halo(plane, x, size_x, x_halo, y_halo, z_halo)


VMEM = pl.BlockSpec(memory_space=pltpu.VMEM)
SMEM = pl.BlockSpec(memory_space=pltpu.SMEM)


def call(kernel, name, inputs, shapes, scratch=(), smem=()):
    return pl.pallas_call(
        kernel,
        name=name,
        out_shape=[jax.ShapeDtypeStruct(s, jnp.float32) for s in shapes],
        in_specs=[SMEM if n in smem else VMEM for n in range(len(inputs))],
        out_specs=[VMEM] * len(shapes),
        scratch_shapes=[pltpu.VMEM(s, jnp.float32) for s in scratch],
        compiler_params=pltpu.CompilerParams(vmem_limit_bytes=8 << 20),
    )(*inputs)


def pair_permutations(sizes, dim):
    count = sizes[dim]
    result = []
    for odd in range(1 if count == 2 and dim != 1 else 2):
        pairs = []
        for place in np.ndindex(*sizes):
            other = list(place)
            step = 1 if place[dim] % 2 == odd else -1
            moved = place[dim] + step
            if dim == 1 or 0 <= moved < count:
                other[dim] = moved % count
            else:
                other[1] = place[1] ^ 1
            pairs.append((int(np.ravel_multi_index(place, sizes)), int(np.ravel_multi_index(other, sizes))))
        result.append(pairs)
    return result


def coarse_by_sums(terms, coarse_inverse):
    shape = terms.shape
    sides = []
    weights = []
    for dim, axis in enumerate(AXES):
        count, at = lax.axis_size(axis), lax.axis_index(axis)
        position = jnp.arange(shape[dim])
        first, last = (False, False) if dim == 1 else (at == 0, at == count - 1)
        weights.append(jnp.stack([coarse_weight(position, shape[dim], first, last, o) for o in (-1, 0, 1)]))
        block = at + jnp.arange(-1, 2)
        block = block % count if dim == 1 else block
        sides.append((block[:, None] == jnp.arange(count)[None, :]).astype(jnp.float32))
    part = jnp.einsum("xyz,ax,by,cz->abc", terms, *weights, precision=HIGHEST) / terms.size
    rhs = jnp.einsum("abc,ai,bj,ck->ijk", part, *sides, precision=HIGHEST)
    rhs = lax.psum(rhs, AXES)
    inverse = lax.all_gather(coarse_inverse, AXES, axis=0, tiled=True)
    value = jnp.dot(inverse, rhs.reshape(-1), precision=HIGHEST).reshape(rhs.shape)
    near = jnp.einsum("ijk,ai,bj,ck->abc", value, *sides, precision=HIGHEST)
    classes = weights[0][:, jnp.array([0, 1, shape[0] - 1])]
    return jnp.einsum("abc,ax,by,cz->xyz", near, classes, weights[1], weights[2], precision=HIGHEST)


def on_device(sizes, fluidity, local_fluidity, element_coef, fdm_basis, fdm_values, coarse_inverse):
    shape = size_x, size_y, size_z = fluidity.shape
    gossip = sizes == (2, 4, 4)
    extra_rows = NP if gossip else 0
    perms = [pair_permutations(sizes, dim) for dim in range(3)]
    pairs_x = len(perms[0])

    const = np.zeros((size_z + size_y + NP, size_z), np.float32)
    const[:size_z] = np.kron(np.eye(size_z // NP), STIFF.T)
    const[size_z : size_z + size_y, :size_y] = np.kron(np.eye(size_y // NP), STIFF)
    const[size_z + size_y :] = WEIGHTS[:, None] * np.tile(WEIGHTS, size_z // NP)[None, :]

    face_shapes = [(2, size_x, size_z), (2, size_y, LANES)]
    x_shapes = [(size_y + extra_rows, size_z)] * pairs_x
    tab_shapes = [(NP, size_z)] if gossip else []

    def send(payloads, pairs):
        return [lax.ppermute(p, AXES, q) for p, q in zip(payloads, pairs)]

    def exchange(y_faces, z_faces, x_payloads, tab, extra):
        x_got = send(x_payloads, perms[0])
        extra_got = send([tab] * len(extra), extra)
        y_out = call(
            functools.partial(y_kernel, gossip, pairs_x, len(extra)),
            "y_faces",
            [y_faces, tab, *x_got, *extra_got],
            [(size_x + extra_rows, size_z)] * 2 + tab_shapes,
        )
        y_got = send(y_out[:2], perms[1])
        tab = y_out[-1] if gossip else tab
        z_out = call(
            functools.partial(z_kernel, gossip, pairs_x),
            "z_faces",
            [z_faces, tab, *x_got, *y_got],
            [(size_y + 2 * extra_rows, LANES)] * 2 + tab_shapes,
        )
        z_got = send(z_out[:2], perms[2])
        tab = z_out[-1] if gossip else tab
        return [*x_got, *y_got, *z_got], tab

    terms, y_faces, z_faces, *rest = call(
        functools.partial(terms_kernel, gossip, pairs_x),
        "terms",
        [fluidity, local_fluidity, element_coef, coarse_inverse, const],
        [shape] + face_shapes + x_shapes + tab_shapes,
    )
    tab = rest[-1]
    extra = [perms[2][0]] if gossip else []
    got, tab = exchange(y_faces, z_faces, rest[:pairs_x], tab, extra)
    values = fdm_values.reshape(1, NP)
    operators = call(
        prepare_kernel,
        "operators",
        [fdm_basis, values, values, element_coef],
        [(size_z, size_z)] * 2 + [(size_y, size_y)] * 2 + [shape],
        smem=(2,),
    )
    solved, y_faces, z_faces, *rest = call(
        functools.partial(solve_kernel, gossip, pairs_x),
        "solve",
        [terms, fdm_basis, *operators, tab, *got],
        [shape] + face_shapes + x_shapes + tab_shapes,
        scratch=[shape],
        smem=(1,),
    )
    got, tab = exchange(y_faces, z_faces, rest[:pairs_x], rest[-1], [])
    coarse = tab if gossip else coarse_by_sums(terms, coarse_inverse)
    return call(
        functools.partial(final_kernel, gossip, pairs_x), "final", [solved, coarse, *got], [shape]
    )[0]


def solution(mesh):
    sizes = tuple(mesh.shape[axis] for axis in AXES)
    return jax.shard_map(
        functools.partial(on_device, sizes),
        mesh=mesh,
        in_specs=(
            P("gx", "gy", "gz"),
            P("gx", "gy", "gz"),
            P("gx", "gy", "gz"),
            P(),
            P(),
            P(("gx", "gy", "gz"), None),
        ),
        out_specs=P("gx", "gy", "gz"),
        check_vma=False,
    )
```

```python
import functools

import jax
import jax.numpy as jnp
import numpy as np
from jax import lax
from jax.experimental import pallas as pl
from jax.experimental.pallas import tpu as pltpu
from jax.sharding import PartitionSpec as P

NP = 8
HALF_WIDTH = 3.0
HIGHEST = lax.Precision.HIGHEST
AXES = ("gx", "gy", "gz")
LANES = 128
GLL_EIGHT = (
    -1.0,
    -0.8717401485096066,
    -0.5917001814331423,
    -0.2092992179024789,
    0.2092992179024789,
    0.5917001814331423,
    0.8717401485096066,
    1.0,
)


def gll_tables():
    degree = NP - 1
    gll_nodes = np.array(GLL_EIGHT)
    previous = np.ones(NP)
    current = gll_nodes * 1.0
    for order in range(2, degree + 1):
        following = ((2 * order - 1) * gll_nodes * current - (order - 1) * previous) / order
        previous = current
        current = following
    weights = 2.0 / (degree * (degree + 1) * current * current)
    identity = np.eye(NP)
    spacing = gll_nodes[:, None] - gll_nodes[None, :] + identity
    derivative = current[:, None] / current[None, :] / spacing * (1.0 - identity)
    end_value = degree * (degree + 1) / 4.0
    end_values = np.concatenate([np.array([-end_value]), np.zeros(NP - 2), np.array([end_value])])
    return weights, derivative + identity * end_values[None, :]


WEIGHTS, DERIVATIVE = gll_tables()
STIFF = (DERIVATIVE.T * WEIGHTS[None, :]) @ DERIVATIVE / WEIGHTS[:, None]


def dot(a, b, contract=((1,), (0,))):
    return lax.dot_general(
        a, b, (contract, ((), ())), precision=HIGHEST, preferred_element_type=jnp.float32
    )


def iota(shape, dim):
    return lax.broadcasted_iota(jnp.int32, shape, dim)


def is_even(axis):
    return lax.rem(lax.axis_index(axis), 2) == 0


def is_last(axis):
    return lax.axis_index(axis) == lax.axis_size(axis) - 1


def low_high(received, axis):
    if len(received) == 1:
        return received[0], received[0]
    even = is_even(axis)
    return jnp.where(even, received[1], received[0]), jnp.where(even, received[0], received[1])


def pair_payloads(low, high, axis, count):
    even = is_even(axis)
    payloads = [jnp.where(even, high, low)]
    if count > 1:
        payloads.append(jnp.where(even, low, high))
    return payloads


def merge(own, received):
    return jnp.where(own == 0.0, received, own)


def coarse_weight(position, length, first, last, offset):
    node = position % NP
    edge = (node == 0) | (node == NP - 1)
    at_low, at_high = position == 0, position == length - 1
    own = jnp.where(edge, jnp.where(at_low | at_high, 1.0, 2.0), 0.5)
    own = jnp.where((at_low & first) | (at_high & last), 0.0, own)
    low = jnp.where(at_low & jnp.logical_not(first), 1.0, 0.0)
    high = jnp.where(at_high & jnp.logical_not(last), 1.0, 0.0)
    return jnp.where(offset == 0, own, jnp.where(offset < 0, low, high))


def z_weights(length, block, shape, position_dim):
    k = lax.axis_index("gz")
    offset = block - k
    value = coarse_weight(iota(shape, position_dim), length, k == 0, is_last("gz"), offset)
    return jnp.where(jnp.abs(offset) <= 1, value, 0.0)


def xy_weights(length_y, shape, y_dim, place, at_x, size_x):
    count = lax.axis_size("gy")
    i, j = lax.axis_index("gx"), lax.axis_index("gy")
    off_x = place // count - i
    off_y = lax.rem(place % count - j + count + 1, count) - 1
    y = coarse_weight(iota(shape, y_dim), length_y, False, False, off_y)
    x = coarse_weight(
        jnp.full(shape, at_x, jnp.int32), size_x, i == 0, is_last("gx"), off_x
    )
    return jnp.where((jnp.abs(off_x) <= 1) & (jnp.abs(off_y) <= 1), x * y, 0.0)


def store_faces(field_ref, yf_ref, zf_ref):
    size_x, size_y, size_z = field_ref.shape
    lane = iota((size_y, LANES), 1)
    low = jnp.zeros((size_y, LANES), jnp.float32)
    high = low
    for x in range(size_x):
        yf_ref[0, x : x + 1, :] = field_ref[x, 0:1, :]
        yf_ref[1, x : x + 1, :] = field_ref[x, size_y - 1 : size_y, :]
        low = jnp.where(lane == x, field_ref[x, :, 0:1], low)
        high = jnp.where(lane == x, field_ref[x, :, size_z - 1 : size_z], high)
    zf_ref[0] = low
    zf_ref[1] = high


def diagonal_blocks(tile, length):
    wide = jnp.concatenate([tile[:, :length]] * (length // NP), axis=0)
    same = iota((length, length), 0) // NP == iota((length, length), 1) // NP
    return jnp.where(same, wide, 0.0)


def const_parts(const_ref, size_y, size_z):
    stiff_z = diagonal_blocks(const_ref[0:NP, :], size_z)
    stiff_y = diagonal_blocks(const_ref[NP : 2 * NP, :], size_y)
    return stiff_z, stiff_y, const_ref[2 * NP : 3 * NP, :]


def pair_planes(axis, size, count):
    even = is_even(axis)
    planes = [jnp.where(even, size - 1, 0), jnp.where(even, 0, size - 1)]
    return planes[:count]


def spread_coef(coef_ref, size_z):
    elements, _, count = coef_ref.shape
    coef = jnp.concatenate([coef_ref[e] for e in range(elements)], axis=0)
    return dot(coef, (iota((count, size_z), 0) == iota((count, size_z), 1) // NP).astype(jnp.float32))


def terms_kernel(gossip, pairs_x, u_ref, l_ref, const_ref, coef_ref, cinv_ref, _, t_ref, yf_ref, zf_ref, *outs):
    size_x, size_y, size_z = u_ref.shape
    stiff_z, stiff_y, mass = const_parts(const_ref, size_y, size_z)
    coef = spread_coef(coef_ref, size_z) * HALF_WIDTH
    t_ref[...] = dot(u_ref[...].reshape(size_x * size_y, size_z), stiff_z).reshape(u_ref.shape)
    for x in range(size_x):
        t_ref[x] += dot(stiff_y, u_ref[x])
    for e in range(size_y // NP):
        rows = slice(e * NP, (e + 1) * NP)
        u = [u_ref[b, rows, :] for b in range(NP)]
        scale = coef[e : e + 1, :]
        for a in range(NP):
            total = t_ref[a, rows, :]
            for b in range(NP):
                total = total + float(STIFF[a, b]) * u[b]
            source = HALF_WIDTH**3 * (l_ref[a, rows, :] - u[a])
            t_ref[a, rows, :] = (float(WEIGHTS[a]) * mass) * (source - scale * total)
    store_faces(t_ref, yf_ref, zf_ref)
    for ref, face in zip(outs, pair_payloads(t_ref[0], t_ref[size_x - 1], "gx", pairs_x)):
        ref[...] = face
    if gossip:
        outs[pairs_x][...] = coarse_tables(t_ref, cinv_ref)


def coarse_tables(t_ref, cinv_ref):
    size_x, size_y, size_z = t_ref.shape
    count_z = lax.axis_size("gz")
    rows = lax.axis_size("gx") * lax.axis_size("gy")
    device = (lax.axis_index("gx") * lax.axis_size("gy") + lax.axis_index("gy")) * count_z + lax.axis_index("gz")
    middle = t_ref[1]
    for x in range(2, size_x - 1):
        middle = middle + t_ref[x]
    total = jnp.zeros((rows, size_z), jnp.float32)
    for at_x, plane in ((0, t_ref[0]), (1, middle), (size_x - 1, t_ref[size_x - 1])):
        w = xy_weights(size_y, (rows, size_y), 1, iota((rows, size_y), 0), at_x, size_x)
        total = total + dot(w, plane)
    lane = iota((size_z, LANES), 1)
    w = z_weights(size_z, lane % count_z, (size_z, LANES), 0)
    points = size_x * size_y * size_z
    part = dot(total, jnp.where(lane // count_z == device, w, 0.0)) / points
    width = rows * count_z
    row = jnp.broadcast_to(cinv_ref[...], (rows, width))
    row = jnp.where(iota((rows, width), 1) // count_z == iota((rows, width), 0), row, 0.0)
    lane = iota((width, LANES), 1)
    place = (lane // count_z == device) & (lane % count_z == iota((width, LANES), 0) % count_z)
    inverse = dot(row, place.astype(jnp.float32))
    return jnp.concatenate([part, inverse], axis=1)


def coarse_weights(size_x, size_z, line_ref, plane_ref, same_ref):
    count_z = lax.axis_size("gz")
    shape = line_ref.shape
    line_ref[...] = z_weights(size_z, (iota(shape, 0) // count_z) % count_z, shape, 1)
    square = same_ref.shape
    same_ref[...] = (iota(square, 0) % count_z == iota(square, 1) % count_z).astype(jnp.float32)
    _, size_y, rows = plane_ref.shape
    for n, at_x in enumerate((0, 1, size_x - 1)):
        plane_ref[n] = xy_weights(size_y, (size_y, rows), 0, iota((size_y, rows), 1), at_x, size_x)


def coarse_planes(tab, line_ref, plane_ref, same_ref):
    count_z = lax.axis_size("gz")
    rows = tab.shape[0]
    rhs = dot(tab[:, :LANES], same_ref[...])
    value = jnp.sum(rhs * tab[:, LANES:], axis=0, keepdims=True)
    value = jnp.broadcast_to(value, (rows, LANES))
    value = jnp.where(iota((rows, LANES), 1) // (count_z * count_z) == iota((rows, LANES), 0), value, 0.0)
    line = dot(value, line_ref[...])
    return [dot(plane_ref[n], line) for n in range(3)]


def y_kernel(gossip, pairs_x, table_in_x, yf_ref, tab_ref, *refs):
    size_x, size_z = yf_ref.shape[1:]
    x_refs, refs = refs[:pairs_x], refs[pairs_x:]
    size_y = x_refs[0].shape[0] - (NP if table_in_x else 0)
    row = iota((size_x, size_z), 0)
    faces = []
    for side, at in ((0, 0), (1, size_y - 1)):
        x_low, x_high = low_high([r[at : at + 1, :] for r in x_refs], "gx")
        face = yf_ref[side]
        faces.append(face + jnp.where(row == 0, x_low, 0.0) + jnp.where(row == size_x - 1, x_high, 0.0))
    for ref, face in zip(refs, pair_payloads(faces[0], faces[1], "gy", 2)):
        ref[0:size_x, :] = face
    if gossip:
        tab = tab_ref[...]
        if table_in_x:
            tab = merge(tab, x_refs[0][size_y:, :])
        refs[0][size_x:, :] = tab
        refs[1][size_x:, :] = tab
        refs[2][...] = tab


def merge_kernel(tab_ref, far_ref, _, out_ref):
    out_ref[...] = merge(tab_ref[...], far_ref[...])


def z_kernel(gossip, pairs_x, zf_ref, tab_ref, *refs):
    size_y = zf_ref.shape[1]
    x_refs, y_refs, refs = refs[:pairs_x], refs[pairs_x : pairs_x + 2], refs[pairs_x + 2 :]
    size_x = y_refs[0].shape[0] - (NP if gossip else 0)
    size_z = y_refs[0].shape[1]
    lane = iota((size_y, LANES), 1)
    row = iota((size_y, LANES), 0)
    diagonal = iota((size_x, LANES), 0) == iota((size_x, LANES), 1)
    faces = []
    for side, at in ((0, 0), (1, size_z - 1)):
        x_low, x_high = low_high([r[0:size_y, at : at + 1] for r in x_refs], "gx")
        y_low, y_high = low_high([r[0:size_x, at : at + 1] for r in y_refs], "gy")
        face = zf_ref[side]
        face = face + jnp.where(lane == 0, x_low, 0.0) + jnp.where(lane == size_x - 1, x_high, 0.0)
        for at_y, column in ((0, y_low), (size_y - 1, y_high)):
            line = jnp.sum(jnp.where(diagonal, column, 0.0), axis=0, keepdims=True)
            face = face + jnp.where(row == at_y, line, 0.0)
        faces.append(face)
    for ref, face in zip(refs, pair_payloads(faces[0], faces[1], "gz", 2)):
        ref[0:size_y, :] = face
    if gossip:
        tab = tab_ref[...]
        for r in y_refs:
            tab = merge(tab, r[size_x:, :])
        for ref in refs[:2]:
            ref[size_y : size_y + NP, :] = tab[:, :LANES]
            ref[size_y + NP :, :] = tab[:, LANES:]
        refs[2][...] = tab


def x_keep(x, size_x):
    if x == 0:
        return lax.axis_index("gx") != 0
    if x == size_x - 1:
        return jnp.logical_not(is_last("gx"))
    return None


def kept(plane, keep):
    return plane if keep is None else jnp.where(keep, plane, 0.0)


def z_keep(lane, size_z):
    return jnp.logical_not(((lane == 0) & (lax.axis_index("gz") == 0)) | ((lane == size_z - 1) & is_last("gz")))


def with_xy_halo(plane, x, size_x, x_halo, y_halo):
    size_y, size_z = plane.shape
    if x == 0:
        plane = plane + x_halo[0]
    if x == size_x - 1:
        plane = plane + x_halo[1]
    row, lane = iota(plane.shape, 0), iota(plane.shape, 1)
    plane = plane + jnp.where(row == 0, y_halo[0][x : x + 1, :], 0.0)
    plane = plane + jnp.where(row == size_y - 1, y_halo[1][x : x + 1, :], 0.0)
    return kept(jnp.where(z_keep(lane, size_z), plane, 0.0), x_keep(x, size_x))


def xy_halos(shape, x_refs, y_refs):
    size_x, size_y, _ = shape
    x_halo = low_high([r[0:size_y, :] for r in x_refs], "gx")
    y_halo = low_high([r[0:size_x, :] for r in y_refs], "gy")
    return x_halo, y_halo


def z_halos(shape, z_refs):
    size_x, size_y, _ = shape
    low, high = low_high([r[0:size_y, :] for r in z_refs], "gz")
    lane = iota((size_y, LANES), 1)
    keep = (lane > 0) | (lax.axis_index("gx") != 0)
    keep = keep & ((lane < size_x - 1) | jnp.logical_not(is_last("gx")))
    low = jnp.where(keep & (lax.axis_index("gz") != 0), low, 0.0)
    high = jnp.where(keep & jnp.logical_not(is_last("gz")), high, 0.0)
    return low, high


def merged_table(tab_ref, z_refs, size_y):
    tab = tab_ref[...]
    for r in z_refs:
        tab = merge(tab, jnp.concatenate([r[size_y : size_y + NP, :], r[size_y + NP :, :]], axis=1))
    return tab


def prepare_kernel(basis_ref, values_ref, coef_ref, _, pz_ref, pzt_ref, py_ref, pyt_ref, px_ref, entry_ref, inv_ref, tile_ref):
    size_x, size_y, size_z = inv_ref.shape
    square = (NP, NP)
    diagonal = iota(square, 0) == iota(square, 1)
    basis = basis_ref[...]
    turned = dot(diagonal.astype(jnp.float32), basis, ((1,), (1,)))
    along_y = jnp.sum(jnp.where(diagonal, values_ref[...], 0.0), axis=1, keepdims=True)

    def repeated(matrix):
        tile_ref[...] = jnp.zeros_like(tile_ref)
        tile_ref[:, 0:NP] = matrix
        tile = tile_ref[...]
        for step in (8, 16, 32, 64):
            tile = tile + pltpu.roll(tile, step, 1)
        return jnp.concatenate([tile] * (size_z // LANES), axis=1)

    plain, flipped = repeated(basis), repeated(turned)
    along_z = repeated(jnp.broadcast_to(values_ref[...], square))

    def folded(length):
        row, col = iota((length, length), 0), iota((length, length), 1)
        wide = diagonal_blocks(plain, length)
        up, down = row // NP + 1 == col // NP, row // NP == col // NP + 1
        wide = wide + jnp.where(up & (row % NP == NP - 1), plain[0:1, :length], 0.0)
        return wide + jnp.where(down & (row % NP == 0), plain[NP - 1 : NP, :length], 0.0)

    def folded_turned(length):
        row, col = iota((length, length), 0), iota((length, length), 1)
        wide = diagonal_blocks(flipped, length)
        up, down = col // NP + 1 == row // NP, col // NP == row // NP + 1
        first = jnp.concatenate([turned[:, 0:1]] * (length // NP), axis=0)
        last = jnp.concatenate([turned[:, NP - 1 : NP]] * (length // NP), axis=0)
        wide = wide + jnp.where(up & (col % NP == NP - 1), first, 0.0)
        return wide + jnp.where(down & (col % NP == 0), last, 0.0)

    pz_ref[...] = folded(size_z)
    pzt_ref[...] = folded_turned(size_z)
    py_ref[...] = folded(size_y)
    pyt_ref[...] = folded_turned(size_y)
    px_ref[...] = diagonal_blocks(plain, LANES)
    for a in range(NP):
        for b in range(NP):
            entry_ref[a * NP + b : a * NP + b + 1, :] = jnp.broadcast_to(basis[a : a + 1, b : b + 1], (1, size_z))
    along = along_y + along_z
    coef = spread_coef(coef_ref, size_z)
    for a in range(NP):
        along_x = values_ref[:, a : a + 1]
        for e in range(size_y // NP):
            inv_ref[a, e * NP : (e + 1) * NP, :] = 1.0 / (coef[e : e + 1, :] * (along + along_x) + 1.0)


def forward_kernel(pairs_x, t_ref, pz_ref, pyt_ref, entry_ref, *refs):
    shape = size_x, size_y, size_z = t_ref.shape
    x_refs, y_refs, (s_ref, scratch) = refs[:pairs_x], refs[pairs_x : pairs_x + 2], refs[pairs_x + 2 :]
    x_halo, y_halo = xy_halos(shape, x_refs, y_refs)
    for x in range(size_x):
        s_ref[x] = dot(pyt_ref[...], with_xy_halo(t_ref[x], x, size_x, x_halo, y_halo))
    scratch[...] = dot(s_ref[...].reshape(size_x * size_y, size_z), pz_ref[...]).reshape(shape)
    for e in range(size_y // NP):
        rows = slice(e * NP, (e + 1) * NP)
        r = [scratch[b, rows, :] for b in range(NP)]
        for a in range(NP):
            total = entry_ref[a : a + 1, :] * r[0]
            for b in range(1, NP):
                total = total + entry_ref[b * NP + a : b * NP + a + 1, :] * r[b]
            s_ref[a, rows, :] = total


def middle_kernel(gossip, pairs_x, s_ref, pz_ref, pzt_ref, py_ref, pyt_ref, px_ref, entry_ref, inv_ref, tab_ref, *refs):
    shape = size_x, size_y, size_z = s_ref.shape
    z_refs, half_ref, outs = refs[:2], refs[2], refs[3:]
    low, high = z_halos(shape, z_refs)
    both = jnp.where(iota((size_y, LANES), 1) < NP, low, pltpu.roll(high, NP, 1))
    both = jnp.where(iota((size_y, LANES), 1) < 2 * NP, both, 0.0)
    both = dot(dot(pyt_ref[...], both), px_ref[...])
    last = (size_x - 1) * NP
    weights = []
    for plane in pair_planes("gx", size_x, pairs_x):
        weights.append([jnp.where(plane == 0, entry_ref[b : b + 1, :], entry_ref[last + b : last + b + 1, :]) for b in range(NP)])
    low_row = pz_ref[0:1, 0:LANES]
    high_row = pz_ref[size_z - 1 : size_z, size_z - LANES :]
    for e in range(size_y // NP):
        rows = slice(e * NP, (e + 1) * NP)
        s = []
        for a in range(NP):
            add_low = both[rows, a : a + 1] * low_row
            add_high = both[rows, NP + a : NP + a + 1] * high_row
            if size_z == 2 * LANES:
                add = jnp.concatenate([add_low, add_high], axis=1)
            else:
                gap = jnp.zeros((NP, size_z - 2 * LANES), jnp.float32)
                add = jnp.concatenate([add_low, gap, add_high], axis=1)
            s.append((s_ref[a, rows, :] + add) * inv_ref[a, rows, :])
            half_ref[a, rows, :] = s[a]
        for ref, row in zip(outs[:pairs_x], weights):
            total = row[0] * s[0]
            for b in range(1, NP):
                total = total + row[b] * s[b]
            ref[rows, :] = total
    for ref in outs[:pairs_x]:
        ref[0:size_y, :] = dot(py_ref[...], dot(ref[0:size_y, :], pzt_ref[...]))
    if gossip:
        tab = merged_table(tab_ref, z_refs, size_y)
        outs[pairs_x][...] = tab
        outs[0][size_y:, :] = tab


def inverse_kernel(half_ref, pzt_ref, py_ref, entry_ref, y_ref, yf_ref, zf_ref, scratch):
    shape = size_x, size_y, size_z = half_ref.shape
    for e in range(size_y // NP):
        rows = slice(e * NP, (e + 1) * NP)
        s = [half_ref[b, rows, :] for b in range(NP)]
        for a in range(NP):
            total = entry_ref[a * NP : a * NP + 1, :] * s[0]
            for b in range(1, NP):
                total = total + entry_ref[a * NP + b : a * NP + b + 1, :] * s[b]
            y_ref[a, rows, :] = total
    scratch[...] = dot(y_ref[...].reshape(size_x * size_y, size_z), pzt_ref[...]).reshape(shape)
    for x in range(size_x):
        y_ref[x] = dot(py_ref[...], scratch[x])
    store_faces(y_ref, yf_ref, zf_ref)


def assemble_kernel(pairs_x, s_ref, *refs):
    shape = s_ref.shape
    x_refs, y_refs, out_ref = refs[:pairs_x], refs[pairs_x : pairs_x + 2], refs[-1]
    x_halo, y_halo = xy_halos(shape, x_refs, y_refs)
    for x in range(shape[0]):
        out_ref[x] = with_xy_halo(s_ref[x], x, shape[0], x_halo, y_halo)


def final_kernel(gossip, s_ref, tab_ref, z_low_ref, z_high_ref, *refs):
    shape = size_x, size_y, size_z = s_ref.shape
    z_refs = (z_low_ref, z_high_ref)
    out_ref, buffer, sems = refs[-3:]
    if gossip:
        coarse = coarse_planes(merged_table(tab_ref, z_refs, size_y), *refs[:3])
    else:
        coarse = [tab_ref[c] for c in range(3)]
    lane = iota((size_y, size_z), 1)
    coarse = [jnp.where(z_keep(lane, size_z), plane, 0.0) for plane in coarse]
    low, high = z_halos(shape, z_refs)
    copies = []
    for x in range(size_x):
        plane = kept(coarse[0 if x == 0 else 2 if x == size_x - 1 else 1], x_keep(x, size_x)) + s_ref[x]
        plane = plane + jnp.where(lane == 0, low[:, x : x + 1], 0.0)
        buffer[x] = plane + jnp.where(lane == size_z - 1, high[:, x : x + 1], 0.0)
        copies.append(pltpu.make_async_copy(buffer.at[x], out_ref.at[x], sems.at[x]))
        copies[-1].start()
    for copy in copies:
        copy.wait()


VMEM = pl.BlockSpec(memory_space=pltpu.VMEM)
FLOPS = {
    "weights": 1_500_000_000,
    "operators": 10_000_000,
    "terms": 1_700_000_000,
    "y_faces": 10_000_000,
    "merge": 100_000_000,
    "z_faces": 100_000_000,
    "forward": 1_100_000_000,
    "middle": 1_200_000_000,
    "inverse": 1_800_000_000,
    "assemble": 100_000_000,
    "final": 1_400_000_000,
}
HBM = pl.BlockSpec(memory_space=pltpu.MemorySpace.HBM)


def call(kernel, name, inputs, shapes, scratch=(), in_spec=VMEM, out_spec=VMEM, grant=8 << 20):
    return pl.pallas_call(
        kernel,
        name=name,
        out_shape=[jax.ShapeDtypeStruct(s, jnp.float32) for s in shapes],
        in_specs=[in_spec] * len(inputs),
        out_specs=[out_spec] * len(shapes),
        scratch_shapes=[pltpu.VMEM(s, jnp.float32) if isinstance(s, tuple) else s for s in scratch],
        compiler_params=pltpu.CompilerParams(vmem_limit_bytes=grant),
        cost_estimate=pl.CostEstimate(flops=FLOPS[name], bytes_accessed=0, transcendentals=0),
    )(*inputs)


def pair_permutations(sizes, dim):
    count = sizes[dim]
    result = []
    for odd in range(1 if count == 2 and dim != 1 else 2):
        pairs = []
        for place in np.ndindex(*sizes):
            other = list(place)
            step = 1 if place[dim] % 2 == odd else -1
            moved = place[dim] + step
            if dim == 1 or 0 <= moved < count:
                other[dim] = moved % count
            else:
                other[1] = place[1] ^ 1
            pairs.append((int(np.ravel_multi_index(place, sizes)), int(np.ravel_multi_index(other, sizes))))
        result.append(pairs)
    return result


def far_pairs(sizes):
    places = list(np.ndindex(*sizes))
    others = [(i, j, k ^ 2) for i, j, k in places]
    return [(int(np.ravel_multi_index(a, sizes)), int(np.ravel_multi_index(b, sizes))) for a, b in zip(places, others)]


def coarse_by_sums(terms, coarse_inverse):
    shape = terms.shape
    sides = []
    weights = []
    for dim, axis in enumerate(AXES):
        count, at = lax.axis_size(axis), lax.axis_index(axis)
        position = jnp.arange(shape[dim])
        first, last = (False, False) if dim == 1 else (at == 0, at == count - 1)
        weights.append(jnp.stack([coarse_weight(position, shape[dim], first, last, o) for o in (-1, 0, 1)]))
        block = at + jnp.arange(-1, 2)
        block = block % count if dim == 1 else block
        sides.append((block[:, None] == jnp.arange(count)[None, :]).astype(jnp.float32))
    part = jnp.einsum("xyz,ax,by,cz->abc", terms, *weights, precision=HIGHEST) / terms.size
    rhs = jnp.einsum("abc,ai,bj,ck->ijk", part, *sides, precision=HIGHEST)
    rhs = lax.psum(rhs, AXES)
    inverse = lax.all_gather(coarse_inverse, AXES, axis=0, tiled=True)
    value = jnp.dot(inverse, rhs.reshape(-1), precision=HIGHEST).reshape(rhs.shape)
    near = jnp.einsum("ijk,ai,bj,ck->abc", value, *sides, precision=HIGHEST)
    classes = weights[0][:, jnp.array([0, 1, shape[0] - 1])]
    return jnp.einsum("abc,ax,by,cz->xyz", near, classes, weights[1], weights[2], precision=HIGHEST)


def on_device(sizes, fluidity, local_fluidity, element_coef, fdm_basis, fdm_values, coarse_inverse):
    shape = size_x, size_y, size_z = fluidity.shape
    gossip = sizes == (2, 4, 4)
    table_rows = NP if gossip else 0
    perms_x, perms_y, perms_z = [pair_permutations(sizes, dim) for dim in range(3)]
    pairs_x = len(perms_x)

    tiles = [np.tile(m, size_z // NP) for m in (STIFF.T, STIFF, WEIGHTS[:, None] * WEIGHTS)]
    const = np.concatenate(tiles).astype(np.float32)

    square_z, square_y = (size_z, size_z), (size_y, size_y)
    face_shapes = [(2, size_x, size_z), (2, size_y, LANES)]
    tab_shapes = [(NP, size_z)] if gossip else []

    def send(payloads, pairs):
        return [lax.ppermute(p, AXES, q) for p, q in zip(payloads, pairs)]

    def y_round(y_faces, x_got, tab, table_in_x):
        out = call(
            functools.partial(y_kernel, gossip, pairs_x, table_in_x),
            "y_faces",
            [y_faces, tab, *x_got],
            [(size_x + table_rows, size_z)] * 2 + tab_shapes,
        )
        return send(out[:2], perms_y), out[-1] if gossip else tab, out[0]

    def z_round(z_faces, x_got, y_got, tab):
        out = call(
            functools.partial(z_kernel, gossip, pairs_x),
            "z_faces",
            [z_faces, tab, *x_got, *y_got],
            [(size_y + 2 * table_rows, LANES)] * 2 + tab_shapes,
        )
        return send(out[:2], perms_z), out[-1] if gossip else tab

    coef = element_coef.reshape(size_y // NP, 1, size_z // NP)
    weights = []
    if gossip:
        weights = call(
            functools.partial(coarse_weights, size_x, size_z),
            "weights",
            [],
            [(LANES, size_z), (3, size_y, sizes[0] * sizes[1]), (LANES, LANES)],
        )
    terms, y_faces, z_faces, *rest = call(
        functools.partial(terms_kernel, gossip, pairs_x),
        "terms",
        [fluidity, local_fluidity, const, coef, coarse_inverse, weights[0] if gossip else coef],
        [shape] + face_shapes + [(size_y, size_z)] * pairs_x + tab_shapes,
    )
    x_got = send(rest[:pairs_x], perms_x)
    tab = rest[-1] if gossip else coef
    far = send([tab], [far_pairs(sizes)]) if gossip else []
    y_got, tab, sent = y_round(y_faces, x_got, tab, False)
    pz, pzt, py, pyt, px, entries, inverse = call(
        prepare_kernel,
        "operators",
        [fdm_basis, fdm_values.reshape(1, NP), coef, sent],
        [square_z, square_z, square_y, square_y, (LANES, LANES), (NP * NP, size_z), shape],
        scratch=[(NP, LANES)],
    )
    if gossip:
        tab = call(merge_kernel, "merge", [tab, far[0], px], tab_shapes)[0]
    z_got, tab = z_round(z_faces, x_got, y_got, tab)
    spectrum = call(
        functools.partial(forward_kernel, pairs_x),
        "forward",
        [terms, pz, pyt, entries, *x_got, *y_got],
        [shape],
        scratch=[shape],
    )[0]
    half, *rest = call(
        functools.partial(middle_kernel, gossip, pairs_x),
        "middle",
        [spectrum, pz, pzt, py, pyt, px, entries, inverse, tab, *z_got],
        [shape] + [(size_y + table_rows, size_z)] * pairs_x + tab_shapes,
    )
    x_got = send(rest[:pairs_x], perms_x)
    solved, y_faces, z_faces = call(
        inverse_kernel, "inverse", [half, pzt, py, entries], [shape] + face_shapes, scratch=[shape]
    )
    y_got, tab, _ = y_round(y_faces, x_got, rest[-1] if gossip else coef, gossip)
    z_got, tab = z_round(z_faces, x_got, y_got, tab)
    solved = call(
        functools.partial(assemble_kernel, pairs_x), "assemble", [solved, *x_got, *y_got], [shape]
    )[0]
    coarse = tab if gossip else coarse_by_sums(terms, coarse_inverse)
    return call(
        functools.partial(final_kernel, gossip),
        "final",
        [solved, coarse, *z_got, *weights],
        [shape],
        scratch=[shape, pltpu.SemaphoreType.DMA((size_x,))],
        out_spec=HBM,
    )[0]


def solution(mesh):
    sizes = tuple(mesh.shape[axis] for axis in AXES)
    return jax.shard_map(
        functools.partial(on_device, sizes),
        mesh=mesh,
        in_specs=(
            P("gx", "gy", "gz"),
            P("gx", "gy", "gz"),
            P("gx", "gy", "gz"),
            P(),
            P(),
            P(("gx", "gy", "gz"), None),
        ),
        out_specs=P("gx", "gy", "gz"),
        check_vma=False,
    )
```

```python
import functools

import jax
import jax.numpy as jnp
import numpy as np
from jax import lax
from jax.experimental import pallas as pl
from jax.experimental.pallas import tpu as pltpu
from jax.sharding import PartitionSpec as P

NP = 8
HALF_WIDTH = 3.0
HIGHEST = lax.Precision.HIGHEST
AXES = ("gx", "gy", "gz")
LANES = 128
GLL_EIGHT = (
    -1.0,
    -0.8717401485096066,
    -0.5917001814331423,
    -0.2092992179024789,
    0.2092992179024789,
    0.5917001814331423,
    0.8717401485096066,
    1.0,
)


def gll_tables():
    degree = NP - 1
    gll_nodes = np.array(GLL_EIGHT)
    previous = np.ones(NP)
    current = gll_nodes * 1.0
    for order in range(2, degree + 1):
        following = ((2 * order - 1) * gll_nodes * current - (order - 1) * previous) / order
        previous = current
        current = following
    weights = 2.0 / (degree * (degree + 1) * current * current)
    identity = np.eye(NP)
    spacing = gll_nodes[:, None] - gll_nodes[None, :] + identity
    derivative = current[:, None] / current[None, :] / spacing * (1.0 - identity)
    end_value = degree * (degree + 1) / 4.0
    end_values = np.concatenate([np.array([-end_value]), np.zeros(NP - 2), np.array([end_value])])
    return weights, derivative + identity * end_values[None, :]


WEIGHTS, DERIVATIVE = gll_tables()
STIFF = (DERIVATIVE.T * WEIGHTS[None, :]) @ DERIVATIVE / WEIGHTS[:, None]


def dot(a, b, contract=((1,), (0,))):
    return lax.dot_general(
        a, b, (contract, ((), ())), precision=HIGHEST, preferred_element_type=jnp.float32
    )


def parts(a):
    high = a.astype(jnp.bfloat16).astype(jnp.float32)
    rest = a - high
    middle = rest.astype(jnp.bfloat16).astype(jnp.float32)
    return jnp.concatenate([high, middle, rest - middle], axis=0)


def dot_weights(a, weights):
    out = jnp.dot(parts(a).astype(jnp.bfloat16), weights.astype(jnp.bfloat16), preferred_element_type=jnp.float32)
    rows = a.shape[0]
    return out[:rows] + out[rows : 2 * rows] + out[2 * rows :]


def weights_dot(weights, a):
    return jnp.dot(weights.astype(jnp.bfloat16), parts(a).astype(jnp.bfloat16), preferred_element_type=jnp.float32)


def iota(shape, dim):
    return lax.broadcasted_iota(jnp.int32, shape, dim)


def is_even(axis):
    return lax.rem(lax.axis_index(axis), 2) == 0


def is_last(axis):
    return lax.axis_index(axis) == lax.axis_size(axis) - 1


def low_high(received, axis):
    if len(received) == 1:
        return received[0], received[0]
    even = is_even(axis)
    return jnp.where(even, received[1], received[0]), jnp.where(even, received[0], received[1])


def pair_payloads(low, high, axis, count):
    even = is_even(axis)
    payloads = [jnp.where(even, high, low)]
    if count > 1:
        payloads.append(jnp.where(even, low, high))
    return payloads


def merge(own, received):
    return jnp.where(own == 0.0, received, own)


def coarse_weight(position, length, first, last, offset):
    node = position % NP
    edge = (node == 0) | (node == NP - 1)
    at_low, at_high = position == 0, position == length - 1
    own = jnp.where(edge, jnp.where(at_low | at_high, 1.0, 2.0), 0.5)
    own = jnp.where((at_low & first) | (at_high & last), 0.0, own)
    low = jnp.where(at_low & jnp.logical_not(first), 1.0, 0.0)
    high = jnp.where(at_high & jnp.logical_not(last), 1.0, 0.0)
    return jnp.where(offset == 0, own, jnp.where(offset < 0, low, high))


def z_weights(length, block, shape, position_dim):
    k = lax.axis_index("gz")
    offset = block - k
    value = coarse_weight(iota(shape, position_dim), length, k == 0, is_last("gz"), offset)
    return jnp.where(jnp.abs(offset) <= 1, value, 0.0)


def xy_weights(size_x, size_y, point, place):
    count = lax.axis_size("gy")
    i, j = lax.axis_index("gx"), lax.axis_index("gy")
    off_x = place // count - i
    off_y = lax.rem(place % count - j + count + 1, count) - 1
    kind = (point // size_y) % 3
    at_x = jnp.where(kind == 0, 0, jnp.where(kind == 1, 1, size_x - 1))
    y = coarse_weight(point % size_y, size_y, False, False, off_y)
    x = coarse_weight(at_x, size_x, i == 0, is_last("gx"), off_x)
    return jnp.where((jnp.abs(off_x) <= 1) & (jnp.abs(off_y) <= 1), x * y, 0.0)


def store_faces(field_ref, yf_ref, zf_ref):
    size_x, size_y, size_z = field_ref.shape
    lane = iota((size_y, LANES), 1)
    low = jnp.zeros((size_y, LANES), jnp.float32)
    high = low
    for x in range(size_x):
        yf_ref[0, x : x + 1, :] = field_ref[x, 0:1, :]
        yf_ref[1, x : x + 1, :] = field_ref[x, size_y - 1 : size_y, :]
        low = jnp.where(lane == x, field_ref[x, :, 0:1], low)
        high = jnp.where(lane == x, field_ref[x, :, size_z - 1 : size_z], high)
    zf_ref[0] = low
    zf_ref[1] = high


def diagonal_blocks(tile, length):
    wide = jnp.concatenate([tile[:, :length]] * (length // NP), axis=0)
    same = iota((length, length), 0) // NP == iota((length, length), 1) // NP
    return jnp.where(same, wide, 0.0)


def const_parts(const_ref, size_y, size_z):
    stiff_z = diagonal_blocks(const_ref[0:NP, :], size_z)
    stiff_y = diagonal_blocks(const_ref[NP : 2 * NP, :], size_y)
    return stiff_z, stiff_y, const_ref[2 * NP : 3 * NP, :]


def pair_planes(axis, size, count):
    even = is_even(axis)
    planes = [jnp.where(even, size - 1, 0), jnp.where(even, 0, size - 1)]
    return planes[:count]


def spread_coef(coef_ref, size_z):
    elements, _, count = coef_ref.shape
    coef = jnp.concatenate([coef_ref[e] for e in range(elements)], axis=0)
    return dot(coef, (iota((count, size_z), 0) == iota((count, size_z), 1) // NP).astype(jnp.float32))


def terms_kernel(gossip, pairs_x, u_ref, l_ref, const_ref, coef_ref, cinv_ref, *refs):
    weights, (t_ref, yf_ref, zf_ref, *outs) = (refs[:3], refs[3:]) if gossip else ((), refs)
    size_x, size_y, size_z = u_ref.shape
    stiff_z, stiff_y, mass = const_parts(const_ref, size_y, size_z)
    coef = spread_coef(coef_ref, size_z) * HALF_WIDTH
    t_ref[...] = dot(u_ref[...].reshape(size_x * size_y, size_z), stiff_z).reshape(u_ref.shape)
    for x in range(size_x):
        t_ref[x] += dot(stiff_y, u_ref[x])
    for e in range(size_y // NP):
        rows = slice(e * NP, (e + 1) * NP)
        u = [u_ref[b, rows, :] for b in range(NP)]
        scale = coef[e : e + 1, :]
        for a in range(NP):
            total = t_ref[a, rows, :]
            for b in range(NP):
                total = total + float(STIFF[a, b]) * u[b]
            source = HALF_WIDTH**3 * (l_ref[a, rows, :] - u[a])
            t_ref[a, rows, :] = (float(WEIGHTS[a]) * mass) * (source - scale * total)
    store_faces(t_ref, yf_ref, zf_ref)
    for ref, face in zip(outs, pair_payloads(t_ref[0], t_ref[size_x - 1], "gx", pairs_x)):
        ref[...] = face
    if gossip:
        outs[pairs_x][...] = coarse_tables(t_ref, cinv_ref, *weights)


def coarse_tables(t_ref, cinv_ref, sum_y_ref, sum_z_ref, place_ref):
    size_x, size_y, size_z = t_ref.shape
    rows, width = sum_y_ref.shape[0], cinv_ref.shape[1]
    middle = t_ref[1]
    for x in range(2, size_x - 1):
        middle = middle + t_ref[x]
    planes = jnp.concatenate([t_ref[0], middle, t_ref[size_x - 1]], axis=0)
    total = weights_dot(sum_y_ref[...], planes)
    part = dot_weights(total, sum_z_ref[...]) / (size_x * size_y * size_z)
    row = jnp.broadcast_to(cinv_ref[...], (rows, width))
    row = jnp.where(iota((rows, width), 1) // (width // rows) == iota((rows, width), 0), row, 0.0)
    return jnp.concatenate([part, dot_weights(row, place_ref[...])], axis=1)


def coarse_weights(size_x, size_z, line_ref, plane_ref, same_ref, sum_y_ref, sum_z_ref, place_ref):
    count_z = lax.axis_size("gz")
    shape = line_ref.shape
    line_ref[...] = z_weights(size_z, (iota(shape, 0) // count_z) % count_z, shape, 1)
    square = same_ref.shape
    same_ref[...] = (iota(square, 0) % count_z == iota(square, 1) % count_z).astype(jnp.float32)
    size_y = plane_ref.shape[0] // 3
    rows = sum_y_ref.shape[0]
    shape = plane_ref.shape
    plane_ref[...] = xy_weights(size_x, size_y, iota(shape, 0), iota(shape, 1) % rows)
    shape = sum_y_ref.shape
    sum_y_ref[...] = xy_weights(size_x, size_y, iota(shape, 1), iota(shape, 0))
    device = (lax.axis_index("gx") * lax.axis_size("gy") + lax.axis_index("gy")) * count_z + lax.axis_index("gz")
    lane = iota((size_z, LANES), 1)
    w = z_weights(size_z, lane % count_z, (size_z, LANES), 0)
    sum_z_ref[...] = jnp.where(lane // count_z == device, w, 0.0)
    shape = place_ref.shape
    lane = iota(shape, 1)
    place = (lane // count_z == device) & (lane % count_z == iota(shape, 0) % count_z)
    place_ref[...] = place.astype(jnp.float32)


def coarse_planes(tab, line_ref, plane_ref, same_ref):
    count_z = lax.axis_size("gz")
    rows = tab.shape[0]
    rhs = dot_weights(tab[:, :LANES], same_ref[...])
    value = jnp.sum(rhs * tab[:, LANES:], axis=0, keepdims=True)
    value = jnp.broadcast_to(value, (rows, LANES))
    value = jnp.where(iota((rows, LANES), 1) // (count_z * count_z) == iota((rows, LANES), 0), value, 0.0)
    planes = weights_dot(plane_ref[...], dot_weights(value, line_ref[...]))
    size_y = plane_ref.shape[0] // 3
    return [planes[n * size_y : (n + 1) * size_y] for n in range(3)]


def y_kernel(gossip, pairs_x, table_in_x, yf_ref, tab_ref, *refs):
    size_x, size_z = yf_ref.shape[1:]
    x_refs, refs = refs[:pairs_x], refs[pairs_x:]
    size_y = x_refs[0].shape[0] - (NP if table_in_x else 0)
    row = iota((size_x, size_z), 0)
    faces = []
    for side, at in ((0, 0), (1, size_y - 1)):
        x_low, x_high = low_high([r[at : at + 1, :] for r in x_refs], "gx")
        face = yf_ref[side]
        faces.append(face + jnp.where(row == 0, x_low, 0.0) + jnp.where(row == size_x - 1, x_high, 0.0))
    for ref, face in zip(refs, pair_payloads(faces[0], faces[1], "gy", 2)):
        ref[0:size_x, :] = face
    if gossip:
        tab = tab_ref[...]
        if table_in_x:
            tab = merge(tab, x_refs[0][size_y:, :])
        refs[0][size_x:, :] = tab
        refs[1][size_x:, :] = tab
        refs[2][...] = tab


def merge_kernel(tab_ref, far_ref, _, out_ref):
    out_ref[...] = merge(tab_ref[...], far_ref[...])


def z_kernel(gossip, pairs_x, zf_ref, tab_ref, *refs):
    size_y = zf_ref.shape[1]
    x_refs, y_refs, refs = refs[:pairs_x], refs[pairs_x : pairs_x + 2], refs[pairs_x + 2 :]
    size_x = y_refs[0].shape[0] - (NP if gossip else 0)
    size_z = y_refs[0].shape[1]
    lane = iota((size_y, LANES), 1)
    row = iota((size_y, LANES), 0)
    diagonal = iota((size_x, LANES), 0) == iota((size_x, LANES), 1)
    faces = []
    for side, at in ((0, 0), (1, size_z - 1)):
        x_low, x_high = low_high([r[0:size_y, at : at + 1] for r in x_refs], "gx")
        y_low, y_high = low_high([r[0:size_x, at : at + 1] for r in y_refs], "gy")
        face = zf_ref[side]
        face = face + jnp.where(lane == 0, x_low, 0.0) + jnp.where(lane == size_x - 1, x_high, 0.0)
        for at_y, column in ((0, y_low), (size_y - 1, y_high)):
            line = jnp.sum(jnp.where(diagonal, column, 0.0), axis=0, keepdims=True)
            face = face + jnp.where(row == at_y, line, 0.0)
        faces.append(face)
    for ref, face in zip(refs, pair_payloads(faces[0], faces[1], "gz", 2)):
        ref[0:size_y, :] = face
    if gossip:
        tab = tab_ref[...]
        for r in y_refs:
            tab = merge(tab, r[size_x:, :])
        for ref in refs[:2]:
            ref[size_y : size_y + NP, :] = tab[:, :LANES]
            ref[size_y + NP :, :] = tab[:, LANES:]
        refs[2][...] = tab


def x_keep(x, size_x):
    if x == 0:
        return lax.axis_index("gx") != 0
    if x == size_x - 1:
        return jnp.logical_not(is_last("gx"))
    return None


def kept(plane, keep):
    return plane if keep is None else jnp.where(keep, plane, 0.0)


def z_keep(lane, size_z):
    return jnp.logical_not(((lane == 0) & (lax.axis_index("gz") == 0)) | ((lane == size_z - 1) & is_last("gz")))


def with_xy_halo(plane, x, size_x, x_halo, y_halo):
    size_y, size_z = plane.shape
    if x == 0:
        plane = plane + x_halo[0]
    if x == size_x - 1:
        plane = plane + x_halo[1]
    row, lane = iota(plane.shape, 0), iota(plane.shape, 1)
    plane = plane + jnp.where(row == 0, y_halo[0][x : x + 1, :], 0.0)
    plane = plane + jnp.where(row == size_y - 1, y_halo[1][x : x + 1, :], 0.0)
    return kept(jnp.where(z_keep(lane, size_z), plane, 0.0), x_keep(x, size_x))


def xy_halos(shape, x_refs, y_refs):
    size_x, size_y, _ = shape
    x_halo = low_high([r[0:size_y, :] for r in x_refs], "gx")
    y_halo = low_high([r[0:size_x, :] for r in y_refs], "gy")
    return x_halo, y_halo


def z_halos(shape, z_refs):
    size_x, size_y, _ = shape
    low, high = low_high([r[0:size_y, :] for r in z_refs], "gz")
    lane = iota((size_y, LANES), 1)
    keep = (lane > 0) | (lax.axis_index("gx") != 0)
    keep = keep & ((lane < size_x - 1) | jnp.logical_not(is_last("gx")))
    low = jnp.where(keep & (lax.axis_index("gz") != 0), low, 0.0)
    high = jnp.where(keep & jnp.logical_not(is_last("gz")), high, 0.0)
    return low, high


def merged_table(tab_ref, z_refs, size_y):
    tab = tab_ref[...]
    for r in z_refs:
        tab = merge(tab, jnp.concatenate([r[size_y : size_y + NP, :], r[size_y + NP :, :]], axis=1))
    return tab


def prepare_kernel(basis_ref, values_ref, coef_ref, _, pz_ref, pzt_ref, py_ref, pyt_ref, px_ref, entry_ref, inv_ref, tile_ref):
    size_x, size_y, size_z = inv_ref.shape
    square = (NP, NP)
    diagonal = iota(square, 0) == iota(square, 1)
    basis = basis_ref[...]
    turned = dot(diagonal.astype(jnp.float32), basis, ((1,), (1,)))
    along_y = jnp.sum(jnp.where(diagonal, values_ref[...], 0.0), axis=1, keepdims=True)

    def repeated(matrix):
        tile_ref[...] = jnp.zeros_like(tile_ref)
        tile_ref[:, 0:NP] = matrix
        tile = tile_ref[...]
        for step in (8, 16, 32, 64):
            tile = tile + pltpu.roll(tile, step, 1)
        return jnp.concatenate([tile] * (size_z // LANES), axis=1)

    plain, flipped = repeated(basis), repeated(turned)
    along_z = repeated(jnp.broadcast_to(values_ref[...], square))

    def folded(length):
        row, col = iota((length, length), 0), iota((length, length), 1)
        wide = diagonal_blocks(plain, length)
        up, down = row // NP + 1 == col // NP, row // NP == col // NP + 1
        wide = wide + jnp.where(up & (row % NP == NP - 1), plain[0:1, :length], 0.0)
        return wide + jnp.where(down & (row % NP == 0), plain[NP - 1 : NP, :length], 0.0)

    def folded_turned(length):
        row, col = iota((length, length), 0), iota((length, length), 1)
        wide = diagonal_blocks(flipped, length)
        up, down = col // NP + 1 == row // NP, col // NP == row // NP + 1
        first = jnp.concatenate([turned[:, 0:1]] * (length // NP), axis=0)
        last = jnp.concatenate([turned[:, NP - 1 : NP]] * (length // NP), axis=0)
        wide = wide + jnp.where(up & (col % NP == NP - 1), first, 0.0)
        return wide + jnp.where(down & (col % NP == 0), last, 0.0)

    pz_ref[...] = folded(size_z)
    pzt_ref[...] = folded_turned(size_z)
    py_ref[...] = folded(size_y)
    pyt_ref[...] = folded_turned(size_y)
    px_ref[...] = diagonal_blocks(plain, LANES)
    for a in range(NP):
        for b in range(NP):
            entry_ref[a * NP + b : a * NP + b + 1, :] = jnp.broadcast_to(basis[a : a + 1, b : b + 1], (1, size_z))
    along = along_y + along_z
    coef = spread_coef(coef_ref, size_z)
    for a in range(NP):
        along_x = values_ref[:, a : a + 1]
        for e in range(size_y // NP):
            inv_ref[a, e * NP : (e + 1) * NP, :] = 1.0 / (coef[e : e + 1, :] * (along + along_x) + 1.0)


def forward_kernel(pairs_x, t_ref, pz_ref, pyt_ref, entry_ref, *refs):
    shape = size_x, size_y, size_z = t_ref.shape
    x_refs, y_refs, (s_ref, scratch) = refs[:pairs_x], refs[pairs_x : pairs_x + 2], refs[pairs_x + 2 :]
    x_halo, y_halo = xy_halos(shape, x_refs, y_refs)
    for x in range(size_x):
        s_ref[x] = dot(pyt_ref[...], with_xy_halo(t_ref[x], x, size_x, x_halo, y_halo))
    scratch[...] = dot(s_ref[...].reshape(size_x * size_y, size_z), pz_ref[...]).reshape(shape)
    for e in range(size_y // NP):
        rows = slice(e * NP, (e + 1) * NP)
        r = [scratch[b, rows, :] for b in range(NP)]
        for a in range(NP):
            total = entry_ref[a : a + 1, :] * r[0]
            for b in range(1, NP):
                total = total + entry_ref[b * NP + a : b * NP + a + 1, :] * r[b]
            s_ref[a, rows, :] = total


def middle_kernel(gossip, pairs_x, s_ref, pz_ref, pzt_ref, py_ref, pyt_ref, px_ref, entry_ref, inv_ref, tab_ref, *refs):
    shape = size_x, size_y, size_z = s_ref.shape
    z_refs, half_ref, outs = refs[:2], refs[2], refs[3:]
    low, high = z_halos(shape, z_refs)
    both = jnp.where(iota((size_y, LANES), 1) < NP, low, pltpu.roll(high, NP, 1))
    both = jnp.where(iota((size_y, LANES), 1) < 2 * NP, both, 0.0)
    both = dot(dot(pyt_ref[...], both), px_ref[...])
    last = (size_x - 1) * NP
    weights = []
    for plane in pair_planes("gx", size_x, pairs_x):
        weights.append([jnp.where(plane == 0, entry_ref[b : b + 1, :], entry_ref[last + b : last + b + 1, :]) for b in range(NP)])
    low_row = pz_ref[0:1, 0:LANES]
    high_row = pz_ref[size_z - 1 : size_z, size_z - LANES :]
    for e in range(size_y // NP):
        rows = slice(e * NP, (e + 1) * NP)
        s = []
        for a in range(NP):
            add_low = both[rows, a : a + 1] * low_row
            add_high = both[rows, NP + a : NP + a + 1] * high_row
            if size_z == 2 * LANES:
                add = jnp.concatenate([add_low, add_high], axis=1)
            else:
                gap = jnp.zeros((NP, size_z - 2 * LANES), jnp.float32)
                add = jnp.concatenate([add_low, gap, add_high], axis=1)
            s.append((s_ref[a, rows, :] + add) * inv_ref[a, rows, :])
            half_ref[a, rows, :] = s[a]
        for ref, row in zip(outs[:pairs_x], weights):
            total = row[0] * s[0]
            for b in range(1, NP):
                total = total + row[b] * s[b]
            ref[rows, :] = total
    for ref in outs[:pairs_x]:
        ref[0:size_y, :] = dot(py_ref[...], dot(ref[0:size_y, :], pzt_ref[...]))
    if gossip:
        tab = merged_table(tab_ref, z_refs, size_y)
        outs[pairs_x][...] = tab
        outs[0][size_y:, :] = tab


def inverse_kernel(half_ref, pzt_ref, py_ref, entry_ref, y_ref, yf_ref, zf_ref, scratch):
    shape = size_x, size_y, size_z = half_ref.shape
    for e in range(size_y // NP):
        rows = slice(e * NP, (e + 1) * NP)
        s = [half_ref[b, rows, :] for b in range(NP)]
        for a in range(NP):
            total = entry_ref[a * NP : a * NP + 1, :] * s[0]
            for b in range(1, NP):
                total = total + entry_ref[a * NP + b : a * NP + b + 1, :] * s[b]
            y_ref[a, rows, :] = total
    scratch[...] = dot(y_ref[...].reshape(size_x * size_y, size_z), pzt_ref[...]).reshape(shape)
    for x in range(size_x):
        y_ref[x] = dot(py_ref[...], scratch[x])
    store_faces(y_ref, yf_ref, zf_ref)


def assemble_kernel(pairs_x, s_ref, *refs):
    shape = s_ref.shape
    x_refs, y_refs, out_ref = refs[:pairs_x], refs[pairs_x : pairs_x + 2], refs[-1]
    x_halo, y_halo = xy_halos(shape, x_refs, y_refs)
    for x in range(shape[0]):
        out_ref[x] = with_xy_halo(s_ref[x], x, shape[0], x_halo, y_halo)


def final_kernel(gossip, s_ref, tab_ref, z_low_ref, z_high_ref, *refs):
    shape = size_x, size_y, size_z = s_ref.shape
    z_refs = (z_low_ref, z_high_ref)
    out_ref, buffer, sems = refs[-3:]
    if gossip:
        coarse = coarse_planes(merged_table(tab_ref, z_refs, size_y), *refs[:3])
    else:
        coarse = [tab_ref[c] for c in range(3)]
    lane = iota((size_y, size_z), 1)
    coarse = [jnp.where(z_keep(lane, size_z), plane, 0.0) for plane in coarse]
    low, high = z_halos(shape, z_refs)
    copies = []
    for x in range(size_x):
        plane = kept(coarse[0 if x == 0 else 2 if x == size_x - 1 else 1], x_keep(x, size_x)) + s_ref[x]
        plane = plane + jnp.where(lane == 0, low[:, x : x + 1], 0.0)
        buffer[x] = plane + jnp.where(lane == size_z - 1, high[:, x : x + 1], 0.0)
        copies.append(pltpu.make_async_copy(buffer.at[x], out_ref.at[x], sems.at[x]))
        copies[-1].start()
    for copy in copies:
        copy.wait()


VMEM = pl.BlockSpec(memory_space=pltpu.VMEM)
FLOPS = {
    "weights": 1_500_000_000,
    "operators": 10_000_000,
    "terms": 1_700_000_000,
    "y_faces": 10_000_000,
    "merge": 100_000_000,
    "z_faces": 100_000_000,
    "forward": 1_100_000_000,
    "middle": 1_200_000_000,
    "inverse": 1_800_000_000,
    "assemble": 100_000_000,
    "final": 1_400_000_000,
}
HBM = pl.BlockSpec(memory_space=pltpu.MemorySpace.HBM)


def call(kernel, name, inputs, shapes, scratch=(), in_spec=VMEM, out_spec=VMEM, grant=8 << 20):
    return pl.pallas_call(
        kernel,
        name=name,
        out_shape=[jax.ShapeDtypeStruct(s, jnp.float32) for s in shapes],
        in_specs=[in_spec] * len(inputs),
        out_specs=[out_spec] * len(shapes),
        scratch_shapes=[pltpu.VMEM(s, jnp.float32) if isinstance(s, tuple) else s for s in scratch],
        compiler_params=pltpu.CompilerParams(vmem_limit_bytes=grant),
        cost_estimate=pl.CostEstimate(flops=FLOPS[name], bytes_accessed=0, transcendentals=0),
    )(*inputs)


def pair_permutations(sizes, dim):
    count = sizes[dim]
    result = []
    for odd in range(1 if count == 2 and dim != 1 else 2):
        pairs = []
        for place in np.ndindex(*sizes):
            other = list(place)
            step = 1 if place[dim] % 2 == odd else -1
            moved = place[dim] + step
            if dim == 1 or 0 <= moved < count:
                other[dim] = moved % count
            else:
                other[1] = place[1] ^ 1
            pairs.append((int(np.ravel_multi_index(place, sizes)), int(np.ravel_multi_index(other, sizes))))
        result.append(pairs)
    return result


def far_pairs(sizes):
    places = list(np.ndindex(*sizes))
    others = [(i, j, k ^ 2) for i, j, k in places]
    return [(int(np.ravel_multi_index(a, sizes)), int(np.ravel_multi_index(b, sizes))) for a, b in zip(places, others)]


def coarse_by_sums(terms, coarse_inverse):
    shape = terms.shape
    sides = []
    weights = []
    for dim, axis in enumerate(AXES):
        count, at = lax.axis_size(axis), lax.axis_index(axis)
        position = jnp.arange(shape[dim])
        first, last = (False, False) if dim == 1 else (at == 0, at == count - 1)
        weights.append(jnp.stack([coarse_weight(position, shape[dim], first, last, o) for o in (-1, 0, 1)]))
        block = at + jnp.arange(-1, 2)
        block = block % count if dim == 1 else block
        sides.append((block[:, None] == jnp.arange(count)[None, :]).astype(jnp.float32))
    part = jnp.einsum("xyz,ax,by,cz->abc", terms, *weights, precision=HIGHEST) / terms.size
    rhs = jnp.einsum("abc,ai,bj,ck->ijk", part, *sides, precision=HIGHEST)
    rhs = lax.psum(rhs, AXES)
    inverse = lax.all_gather(coarse_inverse, AXES, axis=0, tiled=True)
    value = jnp.dot(inverse, rhs.reshape(-1), precision=HIGHEST).reshape(rhs.shape)
    near = jnp.einsum("ijk,ai,bj,ck->abc", value, *sides, precision=HIGHEST)
    classes = weights[0][:, jnp.array([0, 1, shape[0] - 1])]
    return jnp.einsum("abc,ax,by,cz->xyz", near, classes, weights[1], weights[2], precision=HIGHEST)


def on_device(sizes, fluidity, local_fluidity, element_coef, fdm_basis, fdm_values, coarse_inverse):
    shape = size_x, size_y, size_z = fluidity.shape
    gossip = sizes == (2, 4, 4)
    table_rows = NP if gossip else 0
    perms_x, perms_y, perms_z = [pair_permutations(sizes, dim) for dim in range(3)]
    pairs_x = len(perms_x)

    tiles = [np.tile(m, size_z // NP) for m in (STIFF.T, STIFF, WEIGHTS[:, None] * WEIGHTS)]
    const = np.concatenate(tiles).astype(np.float32)

    square_z, square_y = (size_z, size_z), (size_y, size_y)
    face_shapes = [(2, size_x, size_z), (2, size_y, LANES)]
    tab_shapes = [(NP, size_z)] if gossip else []

    def send(payloads, pairs):
        return [lax.ppermute(p, AXES, q) for p, q in zip(payloads, pairs)]

    def y_round(y_faces, x_got, tab, table_in_x):
        out = call(
            functools.partial(y_kernel, gossip, pairs_x, table_in_x),
            "y_faces",
            [y_faces, tab, *x_got],
            [(size_x + table_rows, size_z)] * 2 + tab_shapes,
        )
        return send(out[:2], perms_y), out[-1] if gossip else tab, out[0]

    def z_round(z_faces, x_got, y_got, tab):
        out = call(
            functools.partial(z_kernel, gossip, pairs_x),
            "z_faces",
            [z_faces, tab, *x_got, *y_got],
            [(size_y + 2 * table_rows, LANES)] * 2 + tab_shapes,
        )
        return send(out[:2], perms_z), out[-1] if gossip else tab

    coef = element_coef.reshape(size_y // NP, 1, size_z // NP)
    weights, rows = [], sizes[0] * sizes[1]
    if gossip:
        weights = call(
            functools.partial(coarse_weights, size_x, size_z),
            "weights",
            [],
            [(LANES, size_z), (3 * size_y, 3 * rows), (LANES, LANES), (rows, 9 * size_y), (size_z, LANES), (rows * sizes[2], LANES)],
        )
    terms, y_faces, z_faces, *rest = call(
        functools.partial(terms_kernel, gossip, pairs_x),
        "terms",
        [fluidity, local_fluidity, const, coef, coarse_inverse, *weights[3:]],
        [shape] + face_shapes + [(size_y, size_z)] * pairs_x + tab_shapes,
    )
    x_got = send(rest[:pairs_x], perms_x)
    tab = rest[-1] if gossip else coef
    far = send([tab], [far_pairs(sizes)]) if gossip else []
    y_got, tab, sent = y_round(y_faces, x_got, tab, False)
    pz, pzt, py, pyt, px, entries, inverse = call(
        prepare_kernel,
        "operators",
        [fdm_basis, fdm_values.reshape(1, NP), coef, sent],
        [square_z, square_z, square_y, square_y, (LANES, LANES), (NP * NP, size_z), shape],
        scratch=[(NP, LANES)],
    )
    if gossip:
        tab = call(merge_kernel, "merge", [tab, far[0], px], tab_shapes)[0]
    z_got, tab = z_round(z_faces, x_got, y_got, tab)
    spectrum = call(
        functools.partial(forward_kernel, pairs_x),
        "forward",
        [terms, pz, pyt, entries, *x_got, *y_got],
        [shape],
        scratch=[shape],
    )[0]
    half, *rest = call(
        functools.partial(middle_kernel, gossip, pairs_x),
        "middle",
        [spectrum, pz, pzt, py, pyt, px, entries, inverse, tab, *z_got],
        [shape] + [(size_y + table_rows, size_z)] * pairs_x + tab_shapes,
    )
    x_got = send(rest[:pairs_x], perms_x)
    solved, y_faces, z_faces = call(
        inverse_kernel, "inverse", [half, pzt, py, entries], [shape] + face_shapes, scratch=[shape]
    )
    y_got, tab, _ = y_round(y_faces, x_got, rest[-1] if gossip else coef, gossip)
    z_got, tab = z_round(z_faces, x_got, y_got, tab)
    solved = call(
        functools.partial(assemble_kernel, pairs_x), "assemble", [solved, *x_got, *y_got], [shape]
    )[0]
    coarse = tab if gossip else coarse_by_sums(terms, coarse_inverse)
    return call(
        functools.partial(final_kernel, gossip),
        "final",
        [solved, coarse, *z_got, *weights[:3]],
        [shape],
        scratch=[shape, pltpu.SemaphoreType.DMA((size_x,))],
        out_spec=HBM,
    )[0]


def solution(mesh):
    sizes = tuple(mesh.shape[axis] for axis in AXES)
    return jax.shard_map(
        functools.partial(on_device, sizes),
        mesh=mesh,
        in_specs=(
            P("gx", "gy", "gz"),
            P("gx", "gy", "gz"),
            P("gx", "gy", "gz"),
            P(),
            P(),
            P(("gx", "gy", "gz"), None),
        ),
        out_specs=P("gx", "gy", "gz"),
        check_vma=False,
    )
```

```python
import functools

import jax
import jax.numpy as jnp
import numpy as np
from jax import lax
from jax.experimental import pallas as pl
from jax.experimental.pallas import tpu as pltpu
from jax.sharding import PartitionSpec as P

NP = 8
HALF_WIDTH = 3.0
HIGHEST = lax.Precision.HIGHEST
AXES = ("gx", "gy", "gz")
LANES = 128
GLL_EIGHT = (
    -1.0,
    -0.8717401485096066,
    -0.5917001814331423,
    -0.2092992179024789,
    0.2092992179024789,
    0.5917001814331423,
    0.8717401485096066,
    1.0,
)


def gll_tables():
    degree = NP - 1
    gll_nodes = np.array(GLL_EIGHT)
    previous = np.ones(NP)
    current = gll_nodes * 1.0
    for order in range(2, degree + 1):
        following = ((2 * order - 1) * gll_nodes * current - (order - 1) * previous) / order
        previous = current
        current = following
    weights = 2.0 / (degree * (degree + 1) * current * current)
    identity = np.eye(NP)
    spacing = gll_nodes[:, None] - gll_nodes[None, :] + identity
    derivative = current[:, None] / current[None, :] / spacing * (1.0 - identity)
    end_value = degree * (degree + 1) / 4.0
    end_values = np.concatenate([np.array([-end_value]), np.zeros(NP - 2), np.array([end_value])])
    return weights, derivative + identity * end_values[None, :]


WEIGHTS, DERIVATIVE = gll_tables()
STIFF = (DERIVATIVE.T * WEIGHTS[None, :]) @ DERIVATIVE / WEIGHTS[:, None]


def dot(a, b, contract=((1,), (0,))):
    return lax.dot_general(
        a, b, (contract, ((), ())), precision=HIGHEST, preferred_element_type=jnp.float32
    )


def parts(a):
    high = a.astype(jnp.bfloat16).astype(jnp.float32)
    rest = a - high
    middle = rest.astype(jnp.bfloat16).astype(jnp.float32)
    return jnp.concatenate([high, middle, rest - middle], axis=0)


def dot_weights(a, weights):
    out = jnp.dot(parts(a).astype(jnp.bfloat16), weights.astype(jnp.bfloat16), preferred_element_type=jnp.float32)
    rows = a.shape[0]
    return out[:rows] + out[rows : 2 * rows] + out[2 * rows :]


def weights_dot(weights, a):
    return jnp.dot(weights.astype(jnp.bfloat16), parts(a).astype(jnp.bfloat16), preferred_element_type=jnp.float32)


def iota(shape, dim):
    return lax.broadcasted_iota(jnp.int32, shape, dim)


def is_even(axis):
    return lax.rem(lax.axis_index(axis), 2) == 0


def is_last(axis):
    return lax.axis_index(axis) == lax.axis_size(axis) - 1


def low_high(received, axis):
    if len(received) == 1:
        return received[0], received[0]
    even = is_even(axis)
    return jnp.where(even, received[1], received[0]), jnp.where(even, received[0], received[1])


def pair_payloads(low, high, axis, count):
    even = is_even(axis)
    payloads = [jnp.where(even, high, low)]
    if count > 1:
        payloads.append(jnp.where(even, low, high))
    return payloads


def merge(own, received):
    return jnp.where(own == 0.0, received, own)


def coarse_weight(position, length, first, last, offset):
    node = position % NP
    edge = (node == 0) | (node == NP - 1)
    at_low, at_high = position == 0, position == length - 1
    own = jnp.where(edge, jnp.where(at_low | at_high, 1.0, 2.0), 0.5)
    own = jnp.where((at_low & first) | (at_high & last), 0.0, own)
    low = jnp.where(at_low & jnp.logical_not(first), 1.0, 0.0)
    high = jnp.where(at_high & jnp.logical_not(last), 1.0, 0.0)
    return jnp.where(offset == 0, own, jnp.where(offset < 0, low, high))


def z_weights(length, block, shape, position_dim):
    k = lax.axis_index("gz")
    offset = block - k
    value = coarse_weight(iota(shape, position_dim), length, k == 0, is_last("gz"), offset)
    return jnp.where(jnp.abs(offset) <= 1, value, 0.0)


def xy_weights(size_x, size_y, point, place):
    count = lax.axis_size("gy")
    i, j = lax.axis_index("gx"), lax.axis_index("gy")
    off_x = place // count - i
    off_y = lax.rem(place % count - j + count + 1, count) - 1
    kind = (point // size_y) % 3
    at_x = jnp.where(kind == 0, 0, jnp.where(kind == 1, 1, size_x - 1))
    y = coarse_weight(point % size_y, size_y, False, False, off_y)
    x = coarse_weight(at_x, size_x, i == 0, is_last("gx"), off_x)
    return jnp.where((jnp.abs(off_x) <= 1) & (jnp.abs(off_y) <= 1), x * y, 0.0)


def store_faces(field_ref, yf_ref, zf_ref):
    size_x, size_y, size_z = field_ref.shape
    lane = iota((size_y, LANES), 1)
    low = jnp.zeros((size_y, LANES), jnp.float32)
    high = low
    for x in range(size_x):
        yf_ref[0, x : x + 1, :] = field_ref[x, 0:1, :]
        yf_ref[1, x : x + 1, :] = field_ref[x, size_y - 1 : size_y, :]
        low = jnp.where(lane == x, field_ref[x, :, 0:1], low)
        high = jnp.where(lane == x, field_ref[x, :, size_z - 1 : size_z], high)
    zf_ref[0] = low
    zf_ref[1] = high


def diagonal_blocks(tile, length):
    wide = jnp.concatenate([tile[:, :length]] * (length // NP), axis=0)
    same = iota((length, length), 0) // NP == iota((length, length), 1) // NP
    return jnp.where(same, wide, 0.0)


def const_parts(const_ref, size_y, size_z):
    stiff_z = diagonal_blocks(const_ref[0:NP, :], size_z)
    stiff_y = diagonal_blocks(const_ref[NP : 2 * NP, :], size_y)
    return stiff_z, stiff_y, const_ref[2 * NP : 3 * NP, :]


def pair_planes(axis, size, count):
    even = is_even(axis)
    planes = [jnp.where(even, size - 1, 0), jnp.where(even, 0, size - 1)]
    return planes[:count]


def spread_coef(coef_ref, size_z):
    elements, _, count = coef_ref.shape
    coef = jnp.concatenate([coef_ref[e] for e in range(elements)], axis=0)
    return dot(coef, (iota((count, size_z), 0) == iota((count, size_z), 1) // NP).astype(jnp.float32))


def terms_kernel(gossip, pairs_x, u_ref, l_ref, const_ref, coef_ref, cinv_ref, *refs):
    weights, (t_ref, yf_ref, zf_ref, *outs) = (refs[:3], refs[3:]) if gossip else ((), refs)
    size_x, size_y, size_z = u_ref.shape
    stiff_z, stiff_y, mass = const_parts(const_ref, size_y, size_z)
    coef = spread_coef(coef_ref, size_z) * HALF_WIDTH
    t_ref[...] = dot(u_ref[...].reshape(size_x * size_y, size_z), stiff_z).reshape(u_ref.shape)
    for x in range(size_x):
        t_ref[x] += dot(stiff_y, u_ref[x])
    for e in range(size_y // NP):
        rows = slice(e * NP, (e + 1) * NP)
        u = [u_ref[b, rows, :] for b in range(NP)]
        scale = coef[e : e + 1, :]
        for a in range(NP):
            total = t_ref[a, rows, :]
            for b in range(NP):
                total = total + float(STIFF[a, b]) * u[b]
            source = HALF_WIDTH**3 * (l_ref[a, rows, :] - u[a])
            t_ref[a, rows, :] = (float(WEIGHTS[a]) * mass) * (source - scale * total)
    store_faces(t_ref, yf_ref, zf_ref)
    for ref, face in zip(outs, pair_payloads(t_ref[0], t_ref[size_x - 1], "gx", pairs_x)):
        ref[...] = face
    if gossip:
        outs[pairs_x][...] = coarse_tables(t_ref, cinv_ref, *weights)


def coarse_tables(t_ref, cinv_ref, sum_y_ref, sum_z_ref, place_ref):
    size_x, size_y, size_z = t_ref.shape
    rows, width = sum_y_ref.shape[0], cinv_ref.shape[1]
    middle = t_ref[1]
    for x in range(2, size_x - 1):
        middle = middle + t_ref[x]
    planes = jnp.concatenate([t_ref[0], middle, t_ref[size_x - 1]], axis=0)
    total = weights_dot(sum_y_ref[...], planes)
    part = dot_weights(total, sum_z_ref[...]) / (size_x * size_y * size_z)
    row = jnp.broadcast_to(cinv_ref[...], (rows, width))
    row = jnp.where(iota((rows, width), 1) // (width // rows) == iota((rows, width), 0), row, 0.0)
    return jnp.concatenate([part, dot_weights(row, place_ref[...])], axis=1)


def coarse_weights(size_x, size_z, line_ref, plane_ref, same_ref, sum_y_ref, sum_z_ref, place_ref):
    count_z = lax.axis_size("gz")
    shape = line_ref.shape
    line_ref[...] = z_weights(size_z, (iota(shape, 0) // count_z) % count_z, shape, 1)
    square = same_ref.shape
    same_ref[...] = (iota(square, 0) % count_z == iota(square, 1) % count_z).astype(jnp.float32)
    size_y = plane_ref.shape[0] // 3
    rows = sum_y_ref.shape[0]
    shape = plane_ref.shape
    plane_ref[...] = xy_weights(size_x, size_y, iota(shape, 0), iota(shape, 1) % rows)
    shape = sum_y_ref.shape
    sum_y_ref[...] = xy_weights(size_x, size_y, iota(shape, 1), iota(shape, 0))
    device = (lax.axis_index("gx") * lax.axis_size("gy") + lax.axis_index("gy")) * count_z + lax.axis_index("gz")
    lane = iota((size_z, LANES), 1)
    w = z_weights(size_z, lane % count_z, (size_z, LANES), 0)
    sum_z_ref[...] = jnp.where(lane // count_z == device, w, 0.0)
    shape = place_ref.shape
    lane = iota(shape, 1)
    place = (lane // count_z == device) & (lane % count_z == iota(shape, 0) % count_z)
    place_ref[...] = place.astype(jnp.float32)


def coarse_planes(tab, line_ref, plane_ref, same_ref):
    count_z = lax.axis_size("gz")
    rows = tab.shape[0]
    rhs = dot_weights(tab[:, :LANES], same_ref[...])
    value = jnp.sum(rhs * tab[:, LANES:], axis=0, keepdims=True)
    value = jnp.broadcast_to(value, (rows, LANES))
    value = jnp.where(iota((rows, LANES), 1) // (count_z * count_z) == iota((rows, LANES), 0), value, 0.0)
    planes = weights_dot(plane_ref[...], dot_weights(value, line_ref[...]))
    size_y = plane_ref.shape[0] // 3
    return [planes[n * size_y : (n + 1) * size_y] for n in range(3)]


def y_kernel(gossip, pairs_x, table_in_x, yf_ref, tab_ref, *refs):
    size_x, size_z = yf_ref.shape[1:]
    x_refs, refs = refs[:pairs_x], refs[pairs_x:]
    size_y = x_refs[0].shape[0] - (NP if table_in_x else 0)
    row = iota((size_x, size_z), 0)
    faces = []
    for side, at in ((0, 0), (1, size_y - 1)):
        x_low, x_high = low_high([r[at : at + 1, :] for r in x_refs], "gx")
        face = yf_ref[side]
        faces.append(face + jnp.where(row == 0, x_low, 0.0) + jnp.where(row == size_x - 1, x_high, 0.0))
    for ref, face in zip(refs, pair_payloads(faces[0], faces[1], "gy", 2)):
        ref[0:size_x, :] = face
    if gossip:
        tab = tab_ref[...]
        if table_in_x:
            tab = merge(tab, x_refs[0][size_y:, :])
        refs[0][size_x:, :] = tab
        refs[1][size_x:, :] = tab
        refs[2][...] = tab


def merge_kernel(tab_ref, far_ref, _, out_ref):
    out_ref[...] = merge(tab_ref[...], far_ref[...])


def x_lanes_kept(lane, size_x):
    keep = (lane % NP != 0) | (lax.axis_index("gx") != 0)
    return keep & ((lane % NP != size_x - 1) | jnp.logical_not(is_last("gx"))) & (lane < 2 * NP)


def ahead_kernel(pairs_x, zf_ref, pyt_ref, px_ref, *refs):
    x_refs, out_ref = refs[:pairs_x], refs[-1]
    _, size_y, _ = zf_ref.shape
    size_x, size_z = NP, x_refs[0].shape[1]
    lane = iota((size_y, LANES), 1)
    faces = []
    for side, at in ((0, 0), (1, size_z - 1)):
        x_low, x_high = low_high([r[0:size_y, at : at + 1] for r in x_refs], "gx")
        face = zf_ref[side]
        faces.append(face + jnp.where(lane == 0, x_low, 0.0) + jnp.where(lane == size_x - 1, x_high, 0.0))
    both = jnp.where(lane < NP, faces[0], pltpu.roll(faces[1], NP, 1))
    both = jnp.where(x_lanes_kept(lane, size_x), both, 0.0)
    out_ref[...] = dot(dot(pyt_ref[...], both), px_ref[...])


def transformed_faces(ahead_ref, pyt_ref, px_ref, y_refs, size_x):
    size_y, size_z = ahead_ref.shape[0], y_refs[0].shape[1]
    at_lane = iota((size_x, LANES), 1)
    lines = []
    for side in range(2):
        lines.append(jnp.zeros((1, LANES), jnp.float32))
        for half, at in ((0, 0), (1, size_z - 1)):
            column = low_high([r[0:size_x, at : at + 1] for r in y_refs], "gy")[side]
            here = at_lane == iota((size_x, LANES), 0) + half * NP
            lines[side] = lines[side] + jnp.sum(jnp.where(here, column, 0.0), axis=0, keepdims=True)
    row = iota((NP, LANES), 0)
    pair = jnp.where(row == 0, lines[0], jnp.where(row == 1, lines[1], 0.0))
    pair = jnp.where(x_lanes_kept(iota((NP, LANES), 1), size_x), pair, 0.0)
    pair = dot(pair, px_ref[...])
    both = ahead_ref[...] + pyt_ref[:, 0:1] * pair[0:1, :] + pyt_ref[:, size_y - 1 : size_y] * pair[1:2, :]
    return both, pltpu.roll(both, LANES - NP, 1)


def z_kernel(gossip, pairs_x, transformed, zf_ref, tab_ref, *refs):
    operators, refs = refs[:transformed], refs[transformed:]
    x_refs, y_refs, refs = refs[:pairs_x], refs[pairs_x : pairs_x + 2], refs[pairs_x + 2 :]
    size_x = y_refs[0].shape[0] - (NP if gossip else 0)
    size_z = y_refs[0].shape[1]
    size_y = refs[0].shape[0] - (2 * NP if gossip else 0)
    if transformed:
        faces = transformed_faces(zf_ref, *operators, y_refs, size_x)
    else:
        lane = iota((size_y, LANES), 1)
        row = iota((size_y, LANES), 0)
        diagonal = iota((size_x, LANES), 0) == iota((size_x, LANES), 1)
        faces = []
        for side, at in ((0, 0), (1, size_z - 1)):
            x_low, x_high = low_high([r[0:size_y, at : at + 1] for r in x_refs], "gx")
            y_low, y_high = low_high([r[0:size_x, at : at + 1] for r in y_refs], "gy")
            face = zf_ref[side]
            face = face + jnp.where(lane == 0, x_low, 0.0) + jnp.where(lane == size_x - 1, x_high, 0.0)
            for at_y, column in ((0, y_low), (size_y - 1, y_high)):
                line = jnp.sum(jnp.where(diagonal, column, 0.0), axis=0, keepdims=True)
                face = face + jnp.where(row == at_y, line, 0.0)
            faces.append(face)
    for ref, face in zip(refs, pair_payloads(faces[0], faces[1], "gz", 2)):
        ref[0:size_y, :] = face
    if gossip:
        tab = tab_ref[...]
        for r in y_refs:
            tab = merge(tab, r[size_x:, :])
        for ref in refs[:2]:
            ref[size_y : size_y + NP, :] = tab[:, :LANES]
            ref[size_y + NP :, :] = tab[:, LANES:]
        refs[2][...] = tab


def x_keep(x, size_x):
    if x == 0:
        return lax.axis_index("gx") != 0
    if x == size_x - 1:
        return jnp.logical_not(is_last("gx"))
    return None


def kept(plane, keep):
    return plane if keep is None else jnp.where(keep, plane, 0.0)


def z_keep(lane, size_z):
    return jnp.logical_not(((lane == 0) & (lax.axis_index("gz") == 0)) | ((lane == size_z - 1) & is_last("gz")))


def with_xy_halo(plane, x, size_x, x_halo, y_halo):
    size_y, size_z = plane.shape
    if x == 0:
        plane = plane + x_halo[0]
    if x == size_x - 1:
        plane = plane + x_halo[1]
    row, lane = iota(plane.shape, 0), iota(plane.shape, 1)
    plane = plane + jnp.where(row == 0, y_halo[0][x : x + 1, :], 0.0)
    plane = plane + jnp.where(row == size_y - 1, y_halo[1][x : x + 1, :], 0.0)
    return kept(jnp.where(z_keep(lane, size_z), plane, 0.0), x_keep(x, size_x))


def xy_halos(shape, x_refs, y_refs):
    size_x, size_y, _ = shape
    x_halo = low_high([r[0:size_y, :] for r in x_refs], "gx")
    y_halo = low_high([r[0:size_x, :] for r in y_refs], "gy")
    return x_halo, y_halo


def z_halos(shape, z_refs):
    size_x, size_y, _ = shape
    low, high = low_high([r[0:size_y, :] for r in z_refs], "gz")
    lane = iota((size_y, LANES), 1)
    keep = (lane > 0) | (lax.axis_index("gx") != 0)
    keep = keep & ((lane < size_x - 1) | jnp.logical_not(is_last("gx")))
    low = jnp.where(keep & (lax.axis_index("gz") != 0), low, 0.0)
    high = jnp.where(keep & jnp.logical_not(is_last("gz")), high, 0.0)
    return low, high


def merged_table(tab_ref, z_refs, size_y):
    tab = tab_ref[...]
    for r in z_refs:
        tab = merge(tab, jnp.concatenate([r[size_y : size_y + NP, :], r[size_y + NP :, :]], axis=1))
    return tab


def prepare_kernel(basis_ref, values_ref, coef_ref, _, pz_ref, pzt_ref, py_ref, pyt_ref, px_ref, entry_ref, inv_ref, tile_ref):
    size_x, size_y, size_z = inv_ref.shape
    square = (NP, NP)
    diagonal = iota(square, 0) == iota(square, 1)
    basis = basis_ref[...]
    turned = dot(diagonal.astype(jnp.float32), basis, ((1,), (1,)))
    along_y = jnp.sum(jnp.where(diagonal, values_ref[...], 0.0), axis=1, keepdims=True)

    def repeated(matrix):
        tile_ref[...] = jnp.zeros_like(tile_ref)
        tile_ref[:, 0:NP] = matrix
        tile = tile_ref[...]
        for step in (8, 16, 32, 64):
            tile = tile + pltpu.roll(tile, step, 1)
        return jnp.concatenate([tile] * (size_z // LANES), axis=1)

    plain, flipped = repeated(basis), repeated(turned)
    along_z = repeated(jnp.broadcast_to(values_ref[...], square))

    def folded(length):
        row, col = iota((length, length), 0), iota((length, length), 1)
        wide = diagonal_blocks(plain, length)
        up, down = row // NP + 1 == col // NP, row // NP == col // NP + 1
        wide = wide + jnp.where(up & (row % NP == NP - 1), plain[0:1, :length], 0.0)
        return wide + jnp.where(down & (row % NP == 0), plain[NP - 1 : NP, :length], 0.0)

    def folded_turned(length):
        row, col = iota((length, length), 0), iota((length, length), 1)
        wide = diagonal_blocks(flipped, length)
        up, down = col // NP + 1 == row // NP, col // NP == row // NP + 1
        first = jnp.concatenate([turned[:, 0:1]] * (length // NP), axis=0)
        last = jnp.concatenate([turned[:, NP - 1 : NP]] * (length // NP), axis=0)
        wide = wide + jnp.where(up & (col % NP == NP - 1), first, 0.0)
        return wide + jnp.where(down & (col % NP == 0), last, 0.0)

    pz_ref[...] = folded(size_z)
    pzt_ref[...] = folded_turned(size_z)
    py_ref[...] = folded(size_y)
    pyt_ref[...] = folded_turned(size_y)
    px_ref[...] = diagonal_blocks(plain, LANES)
    for a in range(NP):
        for b in range(NP):
            entry_ref[a * NP + b : a * NP + b + 1, :] = jnp.broadcast_to(basis[a : a + 1, b : b + 1], (1, size_z))
    along = along_y + along_z
    coef = spread_coef(coef_ref, size_z)
    for a in range(NP):
        along_x = values_ref[:, a : a + 1]
        for e in range(size_y // NP):
            inv_ref[a, e * NP : (e + 1) * NP, :] = 1.0 / (coef[e : e + 1, :] * (along + along_x) + 1.0)


def forward_kernel(pairs_x, t_ref, pz_ref, pyt_ref, entry_ref, *refs):
    shape = size_x, size_y, size_z = t_ref.shape
    x_refs, y_refs, (s_ref, scratch) = refs[:pairs_x], refs[pairs_x : pairs_x + 2], refs[pairs_x + 2 :]
    x_halo, y_halo = xy_halos(shape, x_refs, y_refs)
    for x in range(size_x):
        s_ref[x] = dot(pyt_ref[...], with_xy_halo(t_ref[x], x, size_x, x_halo, y_halo))
    scratch[...] = dot(s_ref[...].reshape(size_x * size_y, size_z), pz_ref[...]).reshape(shape)
    for e in range(size_y // NP):
        rows = slice(e * NP, (e + 1) * NP)
        r = [scratch[b, rows, :] for b in range(NP)]
        for a in range(NP):
            total = entry_ref[a : a + 1, :] * r[0]
            for b in range(1, NP):
                total = total + entry_ref[b * NP + a : b * NP + a + 1, :] * r[b]
            s_ref[a, rows, :] = total


def middle_kernel(gossip, pairs_x, s_ref, pz_ref, pzt_ref, py_ref, entry_ref, inv_ref, tab_ref, *refs):
    shape = size_x, size_y, size_z = s_ref.shape
    z_refs, half_ref, outs = refs[:2], refs[2], refs[3:]
    low, high = low_high([r[0:size_y, :] for r in z_refs], "gz")
    low = jnp.where(lax.axis_index("gz") != 0, low, 0.0)
    high = jnp.where(is_last("gz"), 0.0, high)
    both = jnp.where(iota((size_y, LANES), 1) < NP, low, pltpu.roll(high, NP, 1))
    last = (size_x - 1) * NP
    weights = []
    for plane in pair_planes("gx", size_x, pairs_x):
        weights.append([jnp.where(plane == 0, entry_ref[b : b + 1, :], entry_ref[last + b : last + b + 1, :]) for b in range(NP)])
    low_row = pz_ref[0:1, 0:LANES]
    high_row = pz_ref[size_z - 1 : size_z, size_z - LANES :]
    for e in range(size_y // NP):
        rows = slice(e * NP, (e + 1) * NP)
        s = []
        for a in range(NP):
            add_low = both[rows, a : a + 1] * low_row
            add_high = both[rows, NP + a : NP + a + 1] * high_row
            if size_z == 2 * LANES:
                add = jnp.concatenate([add_low, add_high], axis=1)
            else:
                gap = jnp.zeros((NP, size_z - 2 * LANES), jnp.float32)
                add = jnp.concatenate([add_low, gap, add_high], axis=1)
            s.append((s_ref[a, rows, :] + add) * inv_ref[a, rows, :])
            half_ref[a, rows, :] = s[a]
        for ref, row in zip(outs[:pairs_x], weights):
            total = row[0] * s[0]
            for b in range(1, NP):
                total = total + row[b] * s[b]
            ref[rows, :] = total
    for ref in outs[:pairs_x]:
        ref[0:size_y, :] = dot(py_ref[...], dot(ref[0:size_y, :], pzt_ref[...]))
    if gossip:
        tab = merged_table(tab_ref, z_refs, size_y)
        outs[pairs_x][...] = tab
        outs[0][size_y:, :] = tab


def inverse_kernel(half_ref, pzt_ref, py_ref, entry_ref, y_ref, yf_ref, zf_ref, scratch):
    shape = size_x, size_y, size_z = half_ref.shape
    for e in range(size_y // NP):
        rows = slice(e * NP, (e + 1) * NP)
        s = [half_ref[b, rows, :] for b in range(NP)]
        for a in range(NP):
            total = entry_ref[a * NP : a * NP + 1, :] * s[0]
            for b in range(1, NP):
                total = total + entry_ref[a * NP + b : a * NP + b + 1, :] * s[b]
            y_ref[a, rows, :] = total
    scratch[...] = dot(y_ref[...].reshape(size_x * size_y, size_z), pzt_ref[...]).reshape(shape)
    for x in range(size_x):
        y_ref[x] = dot(py_ref[...], scratch[x])
    store_faces(y_ref, yf_ref, zf_ref)


def assemble_kernel(pairs_x, s_ref, *refs):
    shape = s_ref.shape
    x_refs, y_refs, out_ref = refs[:pairs_x], refs[pairs_x : pairs_x + 2], refs[-1]
    x_halo, y_halo = xy_halos(shape, x_refs, y_refs)
    for x in range(shape[0]):
        out_ref[x] = with_xy_halo(s_ref[x], x, shape[0], x_halo, y_halo)


def final_kernel(gossip, s_ref, tab_ref, z_high_ref, z_low_ref, *refs):
    shape = size_x, size_y, size_z = s_ref.shape
    z_refs = (z_low_ref, z_high_ref)
    out_ref, buffer, sems = refs[-3:]
    if gossip:
        coarse = coarse_planes(merged_table(tab_ref, z_refs, size_y), *refs[:3])
    else:
        coarse = [tab_ref[c] for c in range(3)]
    lane = iota((size_y, size_z), 1)
    coarse = [jnp.where(z_keep(lane, size_z), plane, 0.0) for plane in coarse]
    low, high = z_halos(shape, z_refs)
    copies = []
    for x in range(size_x):
        plane = kept(coarse[0 if x == 0 else 2 if x == size_x - 1 else 1], x_keep(x, size_x)) + s_ref[x]
        plane = plane + jnp.where(lane == 0, low[:, x : x + 1], 0.0)
        buffer[x] = plane + jnp.where(lane == size_z - 1, high[:, x : x + 1], 0.0)
        copies.append(pltpu.make_async_copy(buffer.at[x], out_ref.at[x], sems.at[x]))
        copies[-1].start()
    for copy in copies:
        copy.wait()


VMEM = pl.BlockSpec(memory_space=pltpu.VMEM)
FLOPS = {
    "weights": 1_500_000_000,
    "operators": 10_000_000,
    "terms": 1_700_000_000,
    "y_faces": 10_000_000,
    "merge": 100_000_000,
    "ahead": 10_000_000,
    "z_faces": 100_000_000,
    "forward": 1_100_000_000,
    "middle": 1_200_000_000,
    "inverse": 1_800_000_000,
    "assemble": 100_000_000,
    "final": 1_400_000_000,
}
HBM = pl.BlockSpec(memory_space=pltpu.MemorySpace.HBM)


def call(kernel, name, inputs, shapes, scratch=(), in_spec=VMEM, out_spec=VMEM, grant=8 << 20):
    return pl.pallas_call(
        kernel,
        name=name,
        out_shape=[jax.ShapeDtypeStruct(s, jnp.float32) for s in shapes],
        in_specs=[in_spec] * len(inputs),
        out_specs=[out_spec] * len(shapes),
        scratch_shapes=[pltpu.VMEM(s, jnp.float32) if isinstance(s, tuple) else s for s in scratch],
        compiler_params=pltpu.CompilerParams(vmem_limit_bytes=grant),
        cost_estimate=pl.CostEstimate(flops=FLOPS[name], bytes_accessed=0, transcendentals=0),
    )(*inputs)


def pair_permutations(sizes, dim):
    count = sizes[dim]
    result = []
    for odd in range(1 if count == 2 and dim != 1 else 2):
        pairs = []
        for place in np.ndindex(*sizes):
            other = list(place)
            step = 1 if place[dim] % 2 == odd else -1
            moved = place[dim] + step
            if dim == 1 or 0 <= moved < count:
                other[dim] = moved % count
            else:
                other[1] = place[1] ^ 1
            pairs.append((int(np.ravel_multi_index(place, sizes)), int(np.ravel_multi_index(other, sizes))))
        result.append(pairs)
    return result


def far_pairs(sizes):
    places = list(np.ndindex(*sizes))
    others = [(i, j, k ^ 2) for i, j, k in places]
    return [(int(np.ravel_multi_index(a, sizes)), int(np.ravel_multi_index(b, sizes))) for a, b in zip(places, others)]


def coarse_by_sums(terms, coarse_inverse):
    shape = terms.shape
    sides = []
    weights = []
    for dim, axis in enumerate(AXES):
        count, at = lax.axis_size(axis), lax.axis_index(axis)
        position = jnp.arange(shape[dim])
        first, last = (False, False) if dim == 1 else (at == 0, at == count - 1)
        weights.append(jnp.stack([coarse_weight(position, shape[dim], first, last, o) for o in (-1, 0, 1)]))
        block = at + jnp.arange(-1, 2)
        block = block % count if dim == 1 else block
        sides.append((block[:, None] == jnp.arange(count)[None, :]).astype(jnp.float32))
    part = jnp.einsum("xyz,ax,by,cz->abc", terms, *weights, precision=HIGHEST) / terms.size
    rhs = jnp.einsum("abc,ai,bj,ck->ijk", part, *sides, precision=HIGHEST)
    rhs = lax.psum(rhs, AXES)
    inverse = lax.all_gather(coarse_inverse, AXES, axis=0, tiled=True)
    value = jnp.dot(inverse, rhs.reshape(-1), precision=HIGHEST).reshape(rhs.shape)
    near = jnp.einsum("ijk,ai,bj,ck->abc", value, *sides, precision=HIGHEST)
    classes = weights[0][:, jnp.array([0, 1, shape[0] - 1])]
    return jnp.einsum("abc,ax,by,cz->xyz", near, classes, weights[1], weights[2], precision=HIGHEST)


def on_device(sizes, fluidity, local_fluidity, element_coef, fdm_basis, fdm_values, coarse_inverse):
    shape = size_x, size_y, size_z = fluidity.shape
    gossip = sizes == (2, 4, 4)
    table_rows = NP if gossip else 0
    perms_x, perms_y, perms_z = [pair_permutations(sizes, dim) for dim in range(3)]
    pairs_x = len(perms_x)

    tiles = [np.tile(m, size_z // NP) for m in (STIFF.T, STIFF, WEIGHTS[:, None] * WEIGHTS)]
    const = np.concatenate(tiles).astype(np.float32)

    square_z, square_y = (size_z, size_z), (size_y, size_y)
    face_shapes = [(2, size_x, size_z), (2, size_y, LANES)]
    tab_shapes = [(NP, size_z)] if gossip else []

    def send(payloads, pairs):
        return [lax.ppermute(p, AXES, q) for p, q in zip(payloads, pairs)]

    def y_round(y_faces, x_got, tab, table_in_x):
        out = call(
            functools.partial(y_kernel, gossip, pairs_x, table_in_x),
            "y_faces",
            [y_faces, tab, *x_got],
            [(size_x + table_rows, size_z)] * 2 + tab_shapes,
        )
        return send(out[:2], perms_y), out[-1] if gossip else tab, out[0]

    def z_round(z_faces, x_got, y_got, tab, operators=()):
        out = call(
            functools.partial(z_kernel, gossip, pairs_x, len(operators)),
            "z_faces",
            [z_faces, tab, *operators, *x_got, *y_got],
            [(size_y + 2 * table_rows, LANES)] * 2 + tab_shapes,
        )
        return send(out[:2], perms_z), out[-1] if gossip else tab

    coef = element_coef.reshape(size_y // NP, 1, size_z // NP)
    weights, rows = [], sizes[0] * sizes[1]
    if gossip:
        weights = call(
            functools.partial(coarse_weights, size_x, size_z),
            "weights",
            [],
            [(LANES, size_z), (3 * size_y, 3 * rows), (LANES, LANES), (rows, 9 * size_y), (size_z, LANES), (rows * sizes[2], LANES)],
        )
    terms, y_faces, z_faces, *rest = call(
        functools.partial(terms_kernel, gossip, pairs_x),
        "terms",
        [fluidity, local_fluidity, const, coef, coarse_inverse, *weights[3:]],
        [shape] + face_shapes + [(size_y, size_z)] * pairs_x + tab_shapes,
    )
    x_got = send(rest[:pairs_x], perms_x)
    tab = rest[-1] if gossip else coef
    far = send([tab], [far_pairs(sizes)]) if gossip else []
    y_got, tab, sent = y_round(y_faces, x_got, tab, False)
    pz, pzt, py, pyt, px, entries, inverse = call(
        prepare_kernel,
        "operators",
        [fdm_basis, fdm_values.reshape(1, NP), coef, sent],
        [square_z, square_z, square_y, square_y, (LANES, LANES), (NP * NP, size_z), shape],
        scratch=[(NP, LANES)],
    )
    if gossip:
        tab = call(merge_kernel, "merge", [tab, far[0], px], tab_shapes)[0]
    ahead = call(
        functools.partial(ahead_kernel, pairs_x), "ahead", [z_faces, pyt, px, *x_got], [(size_y, LANES)]
    )[0]
    z_got, tab = z_round(ahead, x_got, y_got, tab, (pyt, px))
    spectrum = call(
        functools.partial(forward_kernel, pairs_x),
        "forward",
        [terms, pz, pyt, entries, *x_got, *y_got],
        [shape],
        scratch=[shape],
    )[0]
    half, *rest = call(
        functools.partial(middle_kernel, gossip, pairs_x),
        "middle",
        [spectrum, pz, pzt, py, entries, inverse, tab, *z_got],
        [shape] + [(size_y + table_rows, size_z)] * pairs_x + tab_shapes,
    )
    x_got = send(rest[:pairs_x], perms_x)
    solved, y_faces, z_faces = call(
        inverse_kernel, "inverse", [half, pzt, py, entries], [shape] + face_shapes, scratch=[shape]
    )
    y_got, tab, _ = y_round(y_faces, x_got, rest[-1] if gossip else coef, gossip)
    z_got, tab = z_round(z_faces, x_got, y_got, tab)
    solved = call(
        functools.partial(assemble_kernel, pairs_x), "assemble", [solved, *x_got, *y_got], [shape]
    )[0]
    coarse = tab if gossip else coarse_by_sums(terms, coarse_inverse)
    return call(
        functools.partial(final_kernel, gossip),
        "final",
        [solved, coarse, *z_got[::-1], *weights[:3]],
        [shape],
        scratch=[shape, pltpu.SemaphoreType.DMA((size_x,))],
        out_spec=HBM,
    )[0]


def solution(mesh):
    sizes = tuple(mesh.shape[axis] for axis in AXES)
    return jax.shard_map(
        functools.partial(on_device, sizes),
        mesh=mesh,
        in_specs=(
            P("gx", "gy", "gz"),
            P("gx", "gy", "gz"),
            P("gx", "gy", "gz"),
            P(),
            P(),
            P(("gx", "gy", "gz"), None),
        ),
        out_specs=P("gx", "gy", "gz"),
        check_vma=False,
    )
```

```python
import functools

import jax
import jax.numpy as jnp
import numpy as np
from jax import lax
from jax.experimental import pallas as pl
from jax.experimental.pallas import tpu as pltpu
from jax.sharding import PartitionSpec as P

NP = 8
HALF_WIDTH = 3.0
HIGHEST = lax.Precision.HIGHEST
AXES = ("gx", "gy", "gz")
LANES = 128
GLL_EIGHT = (
    -1.0,
    -0.8717401485096066,
    -0.5917001814331423,
    -0.2092992179024789,
    0.2092992179024789,
    0.5917001814331423,
    0.8717401485096066,
    1.0,
)


def gll_tables():
    degree = NP - 1
    gll_nodes = np.array(GLL_EIGHT)
    previous = np.ones(NP)
    current = gll_nodes * 1.0
    for order in range(2, degree + 1):
        following = ((2 * order - 1) * gll_nodes * current - (order - 1) * previous) / order
        previous = current
        current = following
    weights = 2.0 / (degree * (degree + 1) * current * current)
    identity = np.eye(NP)
    spacing = gll_nodes[:, None] - gll_nodes[None, :] + identity
    derivative = current[:, None] / current[None, :] / spacing * (1.0 - identity)
    end_value = degree * (degree + 1) / 4.0
    end_values = np.concatenate([np.array([-end_value]), np.zeros(NP - 2), np.array([end_value])])
    return weights, derivative + identity * end_values[None, :]


WEIGHTS, DERIVATIVE = gll_tables()
STIFF = (DERIVATIVE.T * WEIGHTS[None, :]) @ DERIVATIVE / WEIGHTS[:, None]


def dot(a, b, contract=((1,), (0,))):
    return lax.dot_general(
        a, b, (contract, ((), ())), precision=HIGHEST, preferred_element_type=jnp.float32
    )


def parts(a):
    high = a.astype(jnp.bfloat16).astype(jnp.float32)
    rest = a - high
    middle = rest.astype(jnp.bfloat16).astype(jnp.float32)
    return jnp.concatenate([high, middle, rest - middle], axis=0)


def dot_weights(a, weights):
    out = jnp.dot(parts(a).astype(jnp.bfloat16), weights.astype(jnp.bfloat16), preferred_element_type=jnp.float32)
    rows = a.shape[0]
    return out[:rows] + out[rows : 2 * rows] + out[2 * rows :]


def weights_dot(weights, a):
    return jnp.dot(weights.astype(jnp.bfloat16), parts(a).astype(jnp.bfloat16), preferred_element_type=jnp.float32)


def iota(shape, dim):
    return lax.broadcasted_iota(jnp.int32, shape, dim)


def is_even(axis):
    return lax.rem(lax.axis_index(axis), 2) == 0


def is_last(axis):
    return lax.axis_index(axis) == lax.axis_size(axis) - 1


def low_high(received, axis):
    if len(received) == 1:
        return received[0], received[0]
    even = is_even(axis)
    return jnp.where(even, received[1], received[0]), jnp.where(even, received[0], received[1])


def pair_payloads(low, high, axis, count):
    even = is_even(axis)
    payloads = [jnp.where(even, high, low)]
    if count > 1:
        payloads.append(jnp.where(even, low, high))
    return payloads


def merge(own, received):
    return jnp.where(own == 0.0, received, own)


def coarse_weight(position, length, first, last, offset):
    node = position % NP
    edge = (node == 0) | (node == NP - 1)
    at_low, at_high = position == 0, position == length - 1
    own = jnp.where(edge, jnp.where(at_low | at_high, 1.0, 2.0), 0.5)
    own = jnp.where((at_low & first) | (at_high & last), 0.0, own)
    low = jnp.where(at_low & jnp.logical_not(first), 1.0, 0.0)
    high = jnp.where(at_high & jnp.logical_not(last), 1.0, 0.0)
    return jnp.where(offset == 0, own, jnp.where(offset < 0, low, high))


def z_weights(length, block, shape, position_dim):
    k = lax.axis_index("gz")
    offset = block - k
    value = coarse_weight(iota(shape, position_dim), length, k == 0, is_last("gz"), offset)
    return jnp.where(jnp.abs(offset) <= 1, value, 0.0)


def xy_weights(size_x, size_y, point, place):
    count = lax.axis_size("gy")
    i, j = lax.axis_index("gx"), lax.axis_index("gy")
    off_x = place // count - i
    off_y = lax.rem(place % count - j + count + 1, count) - 1
    kind = (point // size_y) % 3
    at_x = jnp.where(kind == 0, 0, jnp.where(kind == 1, 1, size_x - 1))
    y = coarse_weight(point % size_y, size_y, False, False, off_y)
    x = coarse_weight(at_x, size_x, i == 0, is_last("gx"), off_x)
    return jnp.where((jnp.abs(off_x) <= 1) & (jnp.abs(off_y) <= 1), x * y, 0.0)


def store_faces(field_ref, yf_ref, zf_ref):
    size_x, size_y, size_z = field_ref.shape
    lane = iota((size_y, LANES), 1)
    low = jnp.zeros((size_y, LANES), jnp.float32)
    high = low
    for x in range(size_x):
        yf_ref[0, x : x + 1, :] = field_ref[x, 0:1, :]
        yf_ref[1, x : x + 1, :] = field_ref[x, size_y - 1 : size_y, :]
        low = jnp.where(lane == x, field_ref[x, :, 0:1], low)
        high = jnp.where(lane == x, field_ref[x, :, size_z - 1 : size_z], high)
    zf_ref[0] = low
    zf_ref[1] = high


def diagonal_blocks(tile, length):
    wide = jnp.concatenate([tile[:, :length]] * (length // NP), axis=0)
    same = iota((length, length), 0) // NP == iota((length, length), 1) // NP
    return jnp.where(same, wide, 0.0)


def const_parts(const_ref, size_y, size_z):
    stiff_z = diagonal_blocks(const_ref[0:NP, :], size_z)
    stiff_y = diagonal_blocks(const_ref[NP : 2 * NP, :], size_y)
    return stiff_z, stiff_y, const_ref[2 * NP : 3 * NP, :]


def pair_planes(axis, size, count):
    even = is_even(axis)
    planes = [jnp.where(even, size - 1, 0), jnp.where(even, 0, size - 1)]
    return planes[:count]


def spread_coef(coef_ref, size_z):
    elements, _, count = coef_ref.shape
    coef = jnp.concatenate([coef_ref[e] for e in range(elements)], axis=0)
    return dot(coef, (iota((count, size_z), 0) == iota((count, size_z), 1) // NP).astype(jnp.float32))


def terms_kernel(gossip, pairs_x, u_ref, l_ref, const_ref, coef_ref, cinv_ref, *refs):
    weights, (t_ref, yf_ref, zf_ref, *outs) = (refs[:3], refs[3:]) if gossip else ((), refs)
    size_x, size_y, size_z = u_ref.shape
    stiff_z, stiff_y, mass = const_parts(const_ref, size_y, size_z)
    coef = spread_coef(coef_ref, size_z) * HALF_WIDTH
    t_ref[...] = dot(u_ref[...].reshape(size_x * size_y, size_z), stiff_z).reshape(u_ref.shape)
    for x in range(size_x):
        t_ref[x] += dot(stiff_y, u_ref[x])
    for e in range(size_y // NP):
        rows = slice(e * NP, (e + 1) * NP)
        u = [u_ref[b, rows, :] for b in range(NP)]
        scale = coef[e : e + 1, :]
        for a in range(NP):
            total = t_ref[a, rows, :]
            for b in range(NP):
                total = total + float(STIFF[a, b]) * u[b]
            source = HALF_WIDTH**3 * (l_ref[a, rows, :] - u[a])
            t_ref[a, rows, :] = (float(WEIGHTS[a]) * mass) * (source - scale * total)
    store_faces(t_ref, yf_ref, zf_ref)
    for ref, face in zip(outs, pair_payloads(t_ref[0], t_ref[size_x - 1], "gx", pairs_x)):
        ref[...] = face
    if gossip:
        outs[pairs_x][...] = coarse_tables(t_ref, cinv_ref, *weights)


def coarse_tables(t_ref, cinv_ref, sum_y_ref, sum_z_ref, place_ref):
    size_x, size_y, size_z = t_ref.shape
    rows, width = sum_y_ref.shape[0], cinv_ref.shape[1]
    middle = t_ref[1]
    for x in range(2, size_x - 1):
        middle = middle + t_ref[x]
    planes = jnp.concatenate([t_ref[0], middle, t_ref[size_x - 1]], axis=0)
    total = weights_dot(sum_y_ref[...], planes)
    part = dot_weights(total, sum_z_ref[...]) / (size_x * size_y * size_z)
    row = jnp.broadcast_to(cinv_ref[...], (rows, width))
    row = jnp.where(iota((rows, width), 1) // (width // rows) == iota((rows, width), 0), row, 0.0)
    return jnp.concatenate([part, dot_weights(row, place_ref[...])], axis=1)


def coarse_weights(size_x, size_z, line_ref, plane_ref, same_ref, sum_y_ref, sum_z_ref, place_ref):
    count_z = lax.axis_size("gz")
    shape = line_ref.shape
    line_ref[...] = z_weights(size_z, (iota(shape, 0) // count_z) % count_z, shape, 1)
    square = same_ref.shape
    same_ref[...] = (iota(square, 0) % count_z == iota(square, 1) % count_z).astype(jnp.float32)
    size_y = plane_ref.shape[0] // 3
    rows = sum_y_ref.shape[0]
    shape = plane_ref.shape
    plane_ref[...] = xy_weights(size_x, size_y, iota(shape, 0), iota(shape, 1) % rows)
    shape = sum_y_ref.shape
    sum_y_ref[...] = xy_weights(size_x, size_y, iota(shape, 1), iota(shape, 0))
    device = (lax.axis_index("gx") * lax.axis_size("gy") + lax.axis_index("gy")) * count_z + lax.axis_index("gz")
    lane = iota((size_z, LANES), 1)
    w = z_weights(size_z, lane % count_z, (size_z, LANES), 0)
    sum_z_ref[...] = jnp.where(lane // count_z == device, w, 0.0)
    shape = place_ref.shape
    lane = iota(shape, 1)
    place = (lane // count_z == device) & (lane % count_z == iota(shape, 0) % count_z)
    place_ref[...] = place.astype(jnp.float32)


def coarse_planes(tab, line_ref, plane_ref, same_ref):
    count_z = lax.axis_size("gz")
    rows = tab.shape[0]
    rhs = dot_weights(tab[:, :LANES], same_ref[...])
    value = jnp.sum(rhs * tab[:, LANES:], axis=0, keepdims=True)
    value = jnp.broadcast_to(value, (rows, LANES))
    value = jnp.where(iota((rows, LANES), 1) // (count_z * count_z) == iota((rows, LANES), 0), value, 0.0)
    planes = weights_dot(plane_ref[...], dot_weights(value, line_ref[...]))
    size_y = plane_ref.shape[0] // 3
    return [planes[n * size_y : (n + 1) * size_y] for n in range(3)]


def y_kernel(gossip, pairs_x, table_in_x, yf_ref, tab_ref, *refs):
    size_x, size_z = yf_ref.shape[1:]
    x_refs, refs = refs[:pairs_x], refs[pairs_x:]
    size_y = x_refs[0].shape[0] - (NP if table_in_x else 0)
    row = iota((size_x, size_z), 0)
    faces = []
    for side, at in ((0, 0), (1, size_y - 1)):
        x_low, x_high = low_high([r[at : at + 1, :] for r in x_refs], "gx")
        face = yf_ref[side]
        faces.append(face + jnp.where(row == 0, x_low, 0.0) + jnp.where(row == size_x - 1, x_high, 0.0))
    for ref, face in zip(refs, pair_payloads(faces[0], faces[1], "gy", 2)):
        ref[0:size_x, :] = face
    if gossip:
        tab = tab_ref[...]
        if table_in_x:
            tab = merge(tab, x_refs[0][size_y:, :])
        refs[0][size_x:, :] = tab
        refs[1][size_x:, :] = tab
        refs[2][...] = tab


def merge_kernel(tab_ref, far_ref, _, out_ref):
    out_ref[...] = merge(tab_ref[...], far_ref[...])


def x_lanes_kept(lane, size_x):
    keep = (lane % NP != 0) | (lax.axis_index("gx") != 0)
    return keep & ((lane % NP != size_x - 1) | jnp.logical_not(is_last("gx"))) & (lane < 2 * NP)


def ahead_kernel(pairs_x, zf_ref, pyt_ref, px_ref, *refs):
    x_refs, out_ref = refs[:pairs_x], refs[-1]
    _, size_y, _ = zf_ref.shape
    size_x, size_z = NP, x_refs[0].shape[1]
    lane = iota((size_y, LANES), 1)
    faces = []
    for side, at in ((0, 0), (1, size_z - 1)):
        x_low, x_high = low_high([r[0:size_y, at : at + 1] for r in x_refs], "gx")
        face = zf_ref[side]
        faces.append(face + jnp.where(lane == 0, x_low, 0.0) + jnp.where(lane == size_x - 1, x_high, 0.0))
    both = jnp.where(lane < NP, faces[0], pltpu.roll(faces[1], NP, 1))
    both = jnp.where(x_lanes_kept(lane, size_x), both, 0.0)
    out_ref[...] = dot(dot(pyt_ref[...], both), px_ref[...])


def transformed_faces(ahead_ref, pyt_ref, px_ref, y_refs, size_x):
    size_y, size_z = ahead_ref.shape[0], y_refs[0].shape[1]
    at_lane = iota((size_x, LANES), 1)
    lines = []
    for side in range(2):
        lines.append(jnp.zeros((1, LANES), jnp.float32))
        for half, at in ((0, 0), (1, size_z - 1)):
            column = low_high([r[0:size_x, at : at + 1] for r in y_refs], "gy")[side]
            here = at_lane == iota((size_x, LANES), 0) + half * NP
            lines[side] = lines[side] + jnp.sum(jnp.where(here, column, 0.0), axis=0, keepdims=True)
    row = iota((NP, LANES), 0)
    pair = jnp.where(row == 0, lines[0], jnp.where(row == 1, lines[1], 0.0))
    pair = jnp.where(x_lanes_kept(iota((NP, LANES), 1), size_x), pair, 0.0)
    pair = dot(pair, px_ref[...])
    both = ahead_ref[...] + pyt_ref[:, 0:1] * pair[0:1, :] + pyt_ref[:, size_y - 1 : size_y] * pair[1:2, :]
    return both, pltpu.roll(both, LANES - NP, 1)


def z_kernel(gossip, pairs_x, transformed, zf_ref, tab_ref, *refs):
    operators, refs = refs[:transformed], refs[transformed:]
    x_refs, y_refs, refs = refs[:pairs_x], refs[pairs_x : pairs_x + 2], refs[pairs_x + 2 :]
    size_x = y_refs[0].shape[0] - (NP if gossip else 0)
    size_z = y_refs[0].shape[1]
    size_y = refs[0].shape[0] - (2 * NP if gossip else 0)
    if transformed:
        faces = transformed_faces(zf_ref, *operators, y_refs, size_x)
    else:
        lane = iota((size_y, LANES), 1)
        row = iota((size_y, LANES), 0)
        diagonal = iota((size_x, LANES), 0) == iota((size_x, LANES), 1)
        faces = []
        for side, at in ((0, 0), (1, size_z - 1)):
            x_low, x_high = low_high([r[0:size_y, at : at + 1] for r in x_refs], "gx")
            y_low, y_high = low_high([r[0:size_x, at : at + 1] for r in y_refs], "gy")
            face = zf_ref[side]
            face = face + jnp.where(lane == 0, x_low, 0.0) + jnp.where(lane == size_x - 1, x_high, 0.0)
            for at_y, column in ((0, y_low), (size_y - 1, y_high)):
                line = jnp.sum(jnp.where(diagonal, column, 0.0), axis=0, keepdims=True)
                face = face + jnp.where(row == at_y, line, 0.0)
            faces.append(face)
    for ref, face in zip(refs, pair_payloads(faces[0], faces[1], "gz", 2)):
        ref[0:size_y, :] = face
    if gossip:
        tab = tab_ref[...]
        for r in y_refs:
            tab = merge(tab, r[size_x:, :])
        for ref in refs[:2]:
            ref[size_y : size_y + NP, :] = tab[:, :LANES]
            ref[size_y + NP :, :] = tab[:, LANES:]
        refs[2][...] = tab


def x_keep(x, size_x):
    if x == 0:
        return lax.axis_index("gx") != 0
    if x == size_x - 1:
        return jnp.logical_not(is_last("gx"))
    return None


def kept(plane, keep):
    return plane if keep is None else jnp.where(keep, plane, 0.0)


def z_keep(lane, size_z):
    return jnp.logical_not(((lane == 0) & (lax.axis_index("gz") == 0)) | ((lane == size_z - 1) & is_last("gz")))


def with_xy_halo(plane, x, size_x, x_halo, y_halo):
    size_y, size_z = plane.shape
    if x == 0:
        plane = plane + x_halo[0]
    if x == size_x - 1:
        plane = plane + x_halo[1]
    row, lane = iota(plane.shape, 0), iota(plane.shape, 1)
    plane = plane + jnp.where(row == 0, y_halo[0][x : x + 1, :], 0.0)
    plane = plane + jnp.where(row == size_y - 1, y_halo[1][x : x + 1, :], 0.0)
    return kept(jnp.where(z_keep(lane, size_z), plane, 0.0), x_keep(x, size_x))


def xy_halos(shape, x_refs, y_refs):
    size_x, size_y, _ = shape
    x_halo = low_high([r[0:size_y, :] for r in x_refs], "gx")
    y_halo = low_high([r[0:size_x, :] for r in y_refs], "gy")
    return x_halo, y_halo


def z_halos(shape, z_refs):
    size_x, size_y, _ = shape
    low, high = low_high([r[0:size_y, :] for r in z_refs], "gz")
    lane = iota((size_y, LANES), 1)
    keep = (lane > 0) | (lax.axis_index("gx") != 0)
    keep = keep & ((lane < size_x - 1) | jnp.logical_not(is_last("gx")))
    low = jnp.where(keep & (lax.axis_index("gz") != 0), low, 0.0)
    high = jnp.where(keep & jnp.logical_not(is_last("gz")), high, 0.0)
    return low, high


def merged_table(tab_ref, z_refs, size_y):
    tab = tab_ref[...]
    for r in z_refs:
        tab = merge(tab, jnp.concatenate([r[size_y : size_y + NP, :], r[size_y + NP :, :]], axis=1))
    return tab


def prepare_kernel(basis_ref, values_ref, coef_ref, _, pz_ref, pzt_ref, py_ref, pyt_ref, px_ref, entry_ref, inv_ref, tile_ref):
    size_x, size_y, size_z = inv_ref.shape
    square = (NP, NP)
    diagonal = iota(square, 0) == iota(square, 1)
    basis = basis_ref[...]
    turned = dot(diagonal.astype(jnp.float32), basis, ((1,), (1,)))
    along_y = jnp.sum(jnp.where(diagonal, values_ref[...], 0.0), axis=1, keepdims=True)

    def repeated(matrix):
        tile_ref[...] = jnp.zeros_like(tile_ref)
        tile_ref[:, 0:NP] = matrix
        tile = tile_ref[...]
        for step in (8, 16, 32, 64):
            tile = tile + pltpu.roll(tile, step, 1)
        return jnp.concatenate([tile] * (size_z // LANES), axis=1)

    plain, flipped = repeated(basis), repeated(turned)
    along_z = repeated(jnp.broadcast_to(values_ref[...], square))

    def folded(length):
        row, col = iota((length, length), 0), iota((length, length), 1)
        wide = diagonal_blocks(plain, length)
        up, down = row // NP + 1 == col // NP, row // NP == col // NP + 1
        wide = wide + jnp.where(up & (row % NP == NP - 1), plain[0:1, :length], 0.0)
        return wide + jnp.where(down & (row % NP == 0), plain[NP - 1 : NP, :length], 0.0)

    def folded_turned(length):
        row, col = iota((length, length), 0), iota((length, length), 1)
        wide = diagonal_blocks(flipped, length)
        up, down = col // NP + 1 == row // NP, col // NP == row // NP + 1
        first = jnp.concatenate([turned[:, 0:1]] * (length // NP), axis=0)
        last = jnp.concatenate([turned[:, NP - 1 : NP]] * (length // NP), axis=0)
        wide = wide + jnp.where(up & (col % NP == NP - 1), first, 0.0)
        return wide + jnp.where(down & (col % NP == 0), last, 0.0)

    pz_ref[...] = folded(size_z)
    pzt_ref[...] = folded_turned(size_z)
    py_ref[...] = folded(size_y)
    pyt_ref[...] = folded_turned(size_y)
    px_ref[...] = diagonal_blocks(plain, LANES)
    for a in range(NP):
        for b in range(NP):
            entry_ref[a * NP + b : a * NP + b + 1, :] = jnp.broadcast_to(basis[a : a + 1, b : b + 1], (1, size_z))
    along = along_y + along_z
    coef = spread_coef(coef_ref, size_z)
    for a in range(NP):
        along_x = values_ref[:, a : a + 1]
        for e in range(size_y // NP):
            inv_ref[a, e * NP : (e + 1) * NP, :] = 1.0 / (coef[e : e + 1, :] * (along + along_x) + 1.0)


def forward_kernel(pairs_x, t_ref, pz_ref, pyt_ref, entry_ref, *refs):
    shape = size_x, size_y, size_z = t_ref.shape
    x_refs, y_refs, (s_ref, scratch) = refs[:pairs_x], refs[pairs_x : pairs_x + 2], refs[pairs_x + 2 :]
    x_halo, y_halo = xy_halos(shape, x_refs, y_refs)
    for x in range(size_x):
        s_ref[x] = dot(pyt_ref[...], with_xy_halo(t_ref[x], x, size_x, x_halo, y_halo))
    scratch[...] = dot(s_ref[...].reshape(size_x * size_y, size_z), pz_ref[...]).reshape(shape)
    for e in range(size_y // NP):
        rows = slice(e * NP, (e + 1) * NP)
        r = [scratch[b, rows, :] for b in range(NP)]
        for a in range(NP):
            total = entry_ref[a : a + 1, :] * r[0]
            for b in range(1, NP):
                total = total + entry_ref[b * NP + a : b * NP + a + 1, :] * r[b]
            s_ref[a, rows, :] = total


def middle_kernel(gossip, pairs_x, s_ref, pz_ref, pzt_ref, py_ref, entry_ref, inv_ref, tab_ref, *refs):
    shape = size_x, size_y, size_z = s_ref.shape
    z_refs, half_ref, outs = refs[:2], refs[2], refs[3:]
    low, high = low_high([r[0:size_y, :] for r in z_refs], "gz")
    low = jnp.where(lax.axis_index("gz") != 0, low, 0.0)
    high = jnp.where(is_last("gz"), 0.0, high)
    both = jnp.where(iota((size_y, LANES), 1) < NP, low, pltpu.roll(high, NP, 1))
    last = (size_x - 1) * NP
    weights = []
    for plane in pair_planes("gx", size_x, pairs_x):
        weights.append([jnp.where(plane == 0, entry_ref[b : b + 1, :], entry_ref[last + b : last + b + 1, :]) for b in range(NP)])
    low_row = pz_ref[0:1, 0:LANES]
    high_row = pz_ref[size_z - 1 : size_z, size_z - LANES :]
    for e in range(size_y // NP):
        rows = slice(e * NP, (e + 1) * NP)
        s = []
        for a in range(NP):
            add_low = both[rows, a : a + 1] * low_row
            add_high = both[rows, NP + a : NP + a + 1] * high_row
            if size_z == 2 * LANES:
                add = jnp.concatenate([add_low, add_high], axis=1)
            else:
                gap = jnp.zeros((NP, size_z - 2 * LANES), jnp.float32)
                add = jnp.concatenate([add_low, gap, add_high], axis=1)
            s.append((s_ref[a, rows, :] + add) * inv_ref[a, rows, :])
            half_ref[a, rows, :] = s[a]
        for ref, row in zip(outs[:pairs_x], weights):
            total = row[0] * s[0]
            for b in range(1, NP):
                total = total + row[b] * s[b]
            ref[rows, :] = total
    for ref in outs[:pairs_x]:
        ref[0:size_y, :] = dot(py_ref[...], dot(ref[0:size_y, :], pzt_ref[...]))
    if gossip:
        tab = merged_table(tab_ref, z_refs, size_y)
        outs[pairs_x][...] = tab
        outs[0][size_y:, :] = tab


def inverse_kernel(half_ref, pzt_ref, py_ref, entry_ref, y_ref, yf_ref, zf_ref, scratch):
    shape = size_x, size_y, size_z = half_ref.shape
    for e in range(size_y // NP):
        rows = slice(e * NP, (e + 1) * NP)
        s = [half_ref[b, rows, :] for b in range(NP)]
        for a in range(NP):
            total = entry_ref[a * NP : a * NP + 1, :] * s[0]
            for b in range(1, NP):
                total = total + entry_ref[a * NP + b : a * NP + b + 1, :] * s[b]
            y_ref[a, rows, :] = total
    scratch[...] = dot(y_ref[...].reshape(size_x * size_y, size_z), pzt_ref[...]).reshape(shape)
    for x in range(size_x):
        y_ref[x] = dot(py_ref[...], scratch[x])
    store_faces(y_ref, yf_ref, zf_ref)


def assemble_kernel(pairs_x, s_ref, *refs):
    shape = s_ref.shape
    x_refs, y_refs, out_ref = refs[:pairs_x], refs[pairs_x : pairs_x + 2], refs[-1]
    x_halo, y_halo = xy_halos(shape, x_refs, y_refs)
    for x in range(shape[0]):
        out_ref[x] = with_xy_halo(s_ref[x], x, shape[0], x_halo, y_halo)


def final_kernel(gossip, s_ref, tab_ref, z_high_ref, z_low_ref, *refs):
    shape = size_x, size_y, size_z = s_ref.shape
    z_refs = (z_low_ref, z_high_ref)
    out_ref, buffer, sems = refs[-3:]
    lane = iota((size_y, size_z), 1)
    low, high = z_halos(shape, z_refs)
    for x in range(size_x):
        plane = s_ref[x] + jnp.where(lane == 0, low[:, x : x + 1], 0.0)
        buffer[x] = plane + jnp.where(lane == size_z - 1, high[:, x : x + 1], 0.0)
    if gossip:
        coarse = coarse_planes(merged_table(tab_ref, z_refs, size_y), *refs[:3])
    else:
        coarse = [tab_ref[c] for c in range(3)]
    copies = []
    for x in range(size_x):
        buffer[x] += coarse[0 if x == 0 else 2 if x == size_x - 1 else 1]
        copies.append(pltpu.make_async_copy(buffer.at[x], out_ref.at[x], sems.at[x]))
        copies[-1].start()
    for copy in copies:
        copy.wait()


VMEM = pl.BlockSpec(memory_space=pltpu.VMEM)
FLOPS = {
    "weights": 1_500_000_000,
    "operators": 10_000_000,
    "terms": 1_700_000_000,
    "y_faces": 10_000_000,
    "merge": 100_000_000,
    "ahead": 10_000_000,
    "z_faces": 100_000_000,
    "forward": 1_100_000_000,
    "middle": 1_200_000_000,
    "inverse": 1_800_000_000,
    "assemble": 100_000_000,
    "final": 1_400_000_000,
}
HBM = pl.BlockSpec(memory_space=pltpu.MemorySpace.HBM)


def call(kernel, name, inputs, shapes, scratch=(), in_spec=VMEM, out_spec=VMEM, grant=8 << 20):
    return pl.pallas_call(
        kernel,
        name=name,
        out_shape=[jax.ShapeDtypeStruct(s, jnp.float32) for s in shapes],
        in_specs=[in_spec] * len(inputs),
        out_specs=[out_spec] * len(shapes),
        scratch_shapes=[pltpu.VMEM(s, jnp.float32) if isinstance(s, tuple) else s for s in scratch],
        compiler_params=pltpu.CompilerParams(vmem_limit_bytes=grant),
        cost_estimate=pl.CostEstimate(flops=FLOPS[name], bytes_accessed=0, transcendentals=0),
    )(*inputs)


def pair_permutations(sizes, dim):
    count = sizes[dim]
    result = []
    for odd in range(1 if count == 2 and dim != 1 else 2):
        pairs = []
        for place in np.ndindex(*sizes):
            other = list(place)
            step = 1 if place[dim] % 2 == odd else -1
            moved = place[dim] + step
            if dim == 1 or 0 <= moved < count:
                other[dim] = moved % count
            else:
                other[1] = place[1] ^ 1
            pairs.append((int(np.ravel_multi_index(place, sizes)), int(np.ravel_multi_index(other, sizes))))
        result.append(pairs)
    return result


def far_pairs(sizes):
    places = list(np.ndindex(*sizes))
    others = [(i, j, k ^ 2) for i, j, k in places]
    return [(int(np.ravel_multi_index(a, sizes)), int(np.ravel_multi_index(b, sizes))) for a, b in zip(places, others)]


def coarse_by_sums(terms, coarse_inverse):
    shape = terms.shape
    sides = []
    weights = []
    for dim, axis in enumerate(AXES):
        count, at = lax.axis_size(axis), lax.axis_index(axis)
        position = jnp.arange(shape[dim])
        first, last = (False, False) if dim == 1 else (at == 0, at == count - 1)
        weights.append(jnp.stack([coarse_weight(position, shape[dim], first, last, o) for o in (-1, 0, 1)]))
        block = at + jnp.arange(-1, 2)
        block = block % count if dim == 1 else block
        sides.append((block[:, None] == jnp.arange(count)[None, :]).astype(jnp.float32))
    part = jnp.einsum("xyz,ax,by,cz->abc", terms, *weights, precision=HIGHEST) / terms.size
    rhs = jnp.einsum("abc,ai,bj,ck->ijk", part, *sides, precision=HIGHEST)
    rhs = lax.psum(rhs, AXES)
    inverse = lax.all_gather(coarse_inverse, AXES, axis=0, tiled=True)
    value = jnp.dot(inverse, rhs.reshape(-1), precision=HIGHEST).reshape(rhs.shape)
    near = jnp.einsum("ijk,ai,bj,ck->abc", value, *sides, precision=HIGHEST)
    classes = weights[0][:, jnp.array([0, 1, shape[0] - 1])]
    return jnp.einsum("abc,ax,by,cz->xyz", near, classes, weights[1], weights[2], precision=HIGHEST)


def on_device(sizes, fluidity, local_fluidity, element_coef, fdm_basis, fdm_values, coarse_inverse):
    shape = size_x, size_y, size_z = fluidity.shape
    gossip = sizes == (2, 4, 4)
    table_rows = NP if gossip else 0
    perms_x, perms_y, perms_z = [pair_permutations(sizes, dim) for dim in range(3)]
    pairs_x = len(perms_x)

    tiles = [np.tile(m, size_z // NP) for m in (STIFF.T, STIFF, WEIGHTS[:, None] * WEIGHTS)]
    const = np.concatenate(tiles).astype(np.float32)

    square_z, square_y = (size_z, size_z), (size_y, size_y)
    face_shapes = [(2, size_x, size_z), (2, size_y, LANES)]
    tab_shapes = [(NP, size_z)] if gossip else []

    def send(payloads, pairs):
        return [lax.ppermute(p, AXES, q) for p, q in zip(payloads, pairs)]

    def y_round(y_faces, x_got, tab, table_in_x):
        out = call(
            functools.partial(y_kernel, gossip, pairs_x, table_in_x),
            "y_faces",
            [y_faces, tab, *x_got],
            [(size_x + table_rows, size_z)] * 2 + tab_shapes,
        )
        return send(out[:2], perms_y), out[-1] if gossip else tab, out[0]

    def z_round(z_faces, x_got, y_got, tab, operators=()):
        out = call(
            functools.partial(z_kernel, gossip, pairs_x, len(operators)),
            "z_faces",
            [z_faces, tab, *operators, *x_got, *y_got],
            [(size_y + 2 * table_rows, LANES)] * 2 + tab_shapes,
        )
        return send(out[:2], perms_z), out[-1] if gossip else tab

    coef = element_coef.reshape(size_y // NP, 1, size_z // NP)
    weights, rows = [], sizes[0] * sizes[1]
    if gossip:
        weights = call(
            functools.partial(coarse_weights, size_x, size_z),
            "weights",
            [],
            [(LANES, size_z), (3 * size_y, 3 * rows), (LANES, LANES), (rows, 9 * size_y), (size_z, LANES), (rows * sizes[2], LANES)],
        )
    terms, y_faces, z_faces, *rest = call(
        functools.partial(terms_kernel, gossip, pairs_x),
        "terms",
        [fluidity, local_fluidity, const, coef, coarse_inverse, *weights[3:]],
        [shape] + face_shapes + [(size_y, size_z)] * pairs_x + tab_shapes,
    )
    x_got = send(rest[:pairs_x], perms_x)
    tab = rest[-1] if gossip else coef
    far = send([tab], [far_pairs(sizes)]) if gossip else []
    y_got, tab, sent = y_round(y_faces, x_got, tab, False)
    pz, pzt, py, pyt, px, entries, inverse = call(
        prepare_kernel,
        "operators",
        [fdm_basis, fdm_values.reshape(1, NP), coef, sent],
        [square_z, square_z, square_y, square_y, (LANES, LANES), (NP * NP, size_z), shape],
        scratch=[(NP, LANES)],
    )
    if gossip:
        tab = call(merge_kernel, "merge", [tab, far[0], px], tab_shapes)[0]
    ahead = call(
        functools.partial(ahead_kernel, pairs_x), "ahead", [z_faces, pyt, px, *x_got], [(size_y, LANES)]
    )[0]
    z_got, tab = z_round(ahead, x_got, y_got, tab, (pyt, px))
    spectrum = call(
        functools.partial(forward_kernel, pairs_x),
        "forward",
        [terms, pz, pyt, entries, *x_got, *y_got],
        [shape],
        scratch=[shape],
    )[0]
    half, *rest = call(
        functools.partial(middle_kernel, gossip, pairs_x),
        "middle",
        [spectrum, pz, pzt, py, entries, inverse, tab, *z_got],
        [shape] + [(size_y + table_rows, size_z)] * pairs_x + tab_shapes,
    )
    x_got = send(rest[:pairs_x], perms_x)
    solved, y_faces, z_faces = call(
        inverse_kernel, "inverse", [half, pzt, py, entries], [shape] + face_shapes, scratch=[shape]
    )
    y_got, tab, _ = y_round(y_faces, x_got, rest[-1] if gossip else coef, gossip)
    z_got, tab = z_round(z_faces, x_got, y_got, tab)
    solved = call(
        functools.partial(assemble_kernel, pairs_x), "assemble", [solved, *x_got, *y_got], [shape]
    )[0]
    coarse = tab if gossip else coarse_by_sums(terms, coarse_inverse)
    return call(
        functools.partial(final_kernel, gossip),
        "final",
        [solved, coarse, *z_got[::-1], *weights[:3]],
        [shape],
        scratch=[shape, pltpu.SemaphoreType.DMA((size_x,))],
        out_spec=HBM,
    )[0]


def solution(mesh):
    sizes = tuple(mesh.shape[axis] for axis in AXES)
    return jax.shard_map(
        functools.partial(on_device, sizes),
        mesh=mesh,
        in_specs=(
            P("gx", "gy", "gz"),
            P("gx", "gy", "gz"),
            P("gx", "gy", "gz"),
            P(),
            P(),
            P(("gx", "gy", "gz"), None),
        ),
        out_specs=P("gx", "gy", "gz"),
        check_vma=False,
    )
```
